128 devices in a mesh: dp: 4 (over z), expert: 32 (over y, x, core).
Axes of the slice: x: 4, y: 4, z: 4, core: 2. Of those that a mesh axis runs over, the one named last changes fastest.
Arguments:
- tokens: bfloat16 [16384, 2048], P(('dp', 'expert')), may hold values from -6 to 6
- grad_mixed: bfloat16 [16384, 2048], P(('dp', 'expert')), may hold values from -0.059814453 to 0.059814453
- expert_ids: int32 [16384, 8], P(('dp', 'expert')), may hold values from 0 to 63, all different within a row; in each aligned block of 128 rows (0 to 127, 128 to 255, ...) at most 32 rows name the same one
- gate_probs: bfloat16 [16384, 8], P(('dp', 'expert')), may hold values from 0.019897461 to 0.25
- gate_proj: bfloat16 [64, 2048, 768], P('expert'), may hold values from -0.125 to 0.125
- up_proj: bfloat16 [64, 2048, 768], P('expert'), may hold values from -0.125 to 0.125
- down_proj: bfloat16 [64, 768, 2048], P('expert'), may hold values from -0.21875 to 0.21875
- share_down: float32 [4, 4, 4], replicated, may hold values from -3 to 3
- share_up: float32 [4, 4, 4], replicated, may hold values from -3 to 3
- factor_down: float32 [64, 4, 512, 16], P('expert'), may hold values from -0.125 to 0.125
- factor_up: float32 [64, 4, 16, 192], P('expert'), may hold values from -0.5 to 0.5
Outputs:
- mixed: bfloat16 [16384, 2048], P(('dp', 'expert'))
- grad_factor_down: float32 [64, 4, 512, 16], P('expert')
- grad_factor_up: float32 [64, 4, 16, 192], P('expert')
- grad_share_down: float32 [4, 4, 4], replicated
- grad_share_up: float32 [4, 4, 4], replicated
The draws below stay inside these ranges and needn't reach their ends.
Inputs may be any that keep to these rules, and one draw needn't show every extreme that they name: `expert_ids`: each row names 8 different experts. In the rows of one device (aligned blocks of 128 rows) no expert is named more than 32 times, a bound that some block reaches.
All inputs are finite; a program needn't handle non-finite values.
Results may differ from the reference program's by a relative error of at most 0.0096.
Values may be sent and summed in bfloat16 or wider, within the bound.
No kernel may reach another device: no remote copies, remote signals or barrier semaphores. Data moves between devices by JAX's collectives and lax.ppermute only.
A program may use at most 192 MiB of HBM per device.

```python
import math
from functools import partial
import jax
import jax.numpy as jnp
import numpy as np
from jax import lax

D = 2048
FF = 768
RANK = 64
KRON = 4
TOP = 8
TOK_DEV = 128
EXPERTS = 64
CAP = 32
TOKENS = 16384
N_DP = 4
N_EXPERT = 32


def block_scale(key, shape, cuts, least, top_value):
    def one(dim, shards_of):
        draws = jax.random.uniform(jax.random.fold_in(jax.random.fold_in(key, 6), dim), (shards_of,), jnp.float32, least / len(cuts), top_value / len(cuts))
        return jnp.repeat(jnp.exp(draws), shape[dim] // shards_of).reshape((-1,) + (1,) * (len(shape) - dim - 1))

    factor_of = one(*cuts[0])
    for cut in cuts[1:]:
        factor_of = factor_of * one(*cut)
    return factor_of


def shared_out(rng, own, number, rows, count, top, bound, slope):
    ranking = jax.random.permutation(rng, count)
    crowded, usual = load_shares(count, rows * top, bound, slope, True), load_shares(count, rows * top, bound, slope, False)
    places = jnp.arange(count)

    def named(tallies, rotation):
        used = int((tallies > 0).sum())
        fixed = max(1, used // 4)
        shifted = fixed + (places - fixed + rotation * (used - fixed)) % max(1, count - fixed)
        return jnp.zeros((count,), jnp.int32).at[ranking[jnp.where(places < fixed, places, shifted)]].set(jnp.asarray(tallies, jnp.int32))

    tallies = jnp.where(number % 4 == 0, named(crowded, number // 4), named(usual, number - number // 4 - 1))
    mixed = jax.random.permutation(jax.random.fold_in(own, 3), count)
    donor, taker = mixed[0:count // 2 * 2:2], mixed[1:count // 2 * 2:2]
    margin = jnp.minimum(tallies[donor] - 1, bound - tallies[taker]) // 2
    margin = jnp.where((donor == ranking[0]) | (taker == ranking[0]) | (tallies[taker] == 0), 0, jnp.maximum(margin, 0))
    shifted = jax.random.randint(jax.random.fold_in(own, 4), (count // 2,), 0, 1 << 20) % (margin + 1)
    tallies = tallies.at[donor].add(-shifted).at[taker].add(shifted)
    labels = jnp.searchsorted(jnp.cumsum(tallies), jnp.arange(rows * top), side="right").astype(jnp.int32)
    listing = labels.reshape(top, rows).T
    listing = listing[jax.random.permutation(jax.random.fold_in(own, 1), rows)]
    rotation = jax.random.randint(jax.random.fold_in(own, 2), (rows, 1), 0, top)
    return jnp.take_along_axis(listing, (jnp.arange(top)[None, :] + rotation) % top, axis=1)


def load_shares(amount, total, limit, slope, full):
    loads = [(1 << 20) // math.isqrt(rank ** slope) + 1 for rank in range(1, amount + 1)]
    largest = limit if full else min(limit, max(-(-total // amount), total * loads[0] // sum(loads)))
    least = 1 if total - largest >= amount - 1 else 0
    given, surplus = [largest] + [least] * (amount - 1), total - largest - least * (amount - 1)
    while surplus > 0:
        free = [i for i in range(1, amount) if given[i] < largest] or [i for i in range(1, amount) if given[i] < limit]
        pool, left = sum([loads[i] for i in free]), surplus
        for i in free:
            more = min(limit - given[i], max(1, left * loads[i] // pool), surplus)
            given[i] = given[i] + more
            surplus = surplus - more
    return np.array(given)


def normal_values(own_key, shape, spread, most, pieces=(), kind=jnp.bfloat16):
    gain = block_scale(own_key, shape, pieces, -0.22, 0.18) if pieces else 1.0
    entries = jax.random.normal(own_key, shape, jnp.float32) * spread * gain
    return jnp.minimum(jnp.maximum(entries, -most), most).astype(kind)


def setup_inputs(seed: int = 0) -> dict:
    key_of = jax.random.split(jax.random.key(seed), 12)
    tokens = normal_values(key_of[0], (TOKENS, D), 1.0, 6.0, ((0, 128),))
    grad_mixed = normal_values(key_of[1], (TOKENS, D), 0.01, 0.059814453, ((0, 128),))
    expert_ids_keys = jax.random.split(jax.random.fold_in(key_of[2], 1), TOKENS // TOK_DEV)
    expert_ids_turns = jax.random.permutation(jax.random.fold_in(key_of[2], 3), TOKENS // TOK_DEV)
    expert_ids = jax.vmap(lambda own, number: shared_out(jax.random.fold_in(key_of[2], 2), own, number, TOK_DEV, EXPERTS, TOP, CAP, 2))(expert_ids_keys, expert_ids_turns).reshape((TOKENS, TOP))
    gate_probs = jnp.clip(0.019897461 + 0.23010254 * jax.random.uniform(key_of[3], (TOKENS, TOP), jnp.float32) ** block_scale(key_of[3], (TOKENS, TOP), ((0, 128),), -0.2, 0.2), 0.019897461, 0.25).astype(jnp.bfloat16)
    gate_proj = normal_values(key_of[4], (EXPERTS, D, FF), D ** -0.5, 0.125, ((0, 32),))
    up_proj = normal_values(key_of[5], (EXPERTS, D, FF), D ** -0.5, 0.125, ((0, 32),))
    down_proj = normal_values(key_of[6], (EXPERTS, FF, D), FF ** -0.5, 0.21875, ((0, 32),))
    share_down = normal_values(key_of[7], (KRON, KRON, KRON), 0.5, 3.0, (), jnp.float32)
    share_up = normal_values(key_of[8], (KRON, KRON, KRON), 0.5, 3.0, (), jnp.float32)
    factor_down = normal_values(key_of[9], (EXPERTS, KRON, D // KRON, RANK // KRON), D ** -0.5, 0.125, ((0, 32),), jnp.float32)
    factor_up = normal_values(key_of[10], (EXPERTS, KRON, RANK // KRON, FF // KRON), (2 * RANK) ** -0.5, 0.5, ((0, 32),), jnp.float32)
    return {"tokens": tokens, "grad_mixed": grad_mixed, "expert_ids": expert_ids, "gate_probs": gate_probs, "gate_proj": gate_proj, "up_proj": up_proj, "down_proj": down_proj, "share_down": share_down, "share_up": share_up, "factor_down": factor_down, "factor_up": factor_up}


def slot_table(ids_block, expert_count, capacity):
    flat_ids = ids_block.reshape(-1).astype(jnp.int32)
    slot_count = flat_ids.shape[0]
    onehot = (flat_ids[:, None] == jnp.arange(expert_count, dtype=jnp.int32)[None, :]).astype(jnp.int32)
    rank_in = jnp.sum((jnp.cumsum(onehot, axis=0) - 1) * onehot, axis=1).astype(jnp.int32)
    position = (flat_ids * capacity + rank_in).astype(jnp.int32)
    slot_map = jnp.full((expert_count * capacity,), slot_count, jnp.int32)
    slot_map = slot_map.at[position].set(jnp.arange(slot_count, dtype=jnp.int32))
    return slot_map, position


def expand(factor_a, factor_b):
    kron_n, rows_b, cols_b = factor_b.shape
    blocks = jnp.einsum("iac,ibd->abcd", factor_a, factor_b, precision=lax.Precision.HIGHEST)
    return blocks.reshape(kron_n * rows_b, kron_n * cols_b)


def factor_grads(factor_a, factor_b, grad_w):
    kron_n, rows_b, cols_b = factor_b.shape
    blocks = grad_w.reshape(kron_n, rows_b, kron_n, cols_b)
    grad_b = jnp.einsum("iac,abcd->ibd", factor_a, blocks, precision=lax.Precision.HIGHEST)
    grad_a = jnp.einsum("ibd,abcd->iac", factor_b, blocks, precision=lax.Precision.HIGHEST)
    return grad_b, grad_a


def expert_forward(row_data, gate_mat, up_mat, down_mat, adapter_down, adapter_up):
    lowrank = jnp.dot(row_data, adapter_down, preferred_element_type=jnp.float32).astype(jnp.bfloat16)
    gate_pre = jnp.dot(row_data, gate_mat, preferred_element_type=jnp.float32) + jnp.dot(lowrank, adapter_up, preferred_element_type=jnp.float32)
    up_pre = jnp.dot(row_data, up_mat, preferred_element_type=jnp.float32)
    hidden = (jax.nn.silu(gate_pre) * up_pre).astype(jnp.bfloat16)
    result = jnp.dot(hidden, down_mat, preferred_element_type=jnp.float32).astype(jnp.bfloat16)
    return result, lowrank, gate_pre, up_pre


def expert_backward(row_data, weighted, down_mat, adapter_up, lowrank, gate_pre, up_pre):
    grad_hidden = jnp.dot(weighted, down_mat.T, preferred_element_type=jnp.float32)
    sigmoid_g = jax.nn.sigmoid(gate_pre)
    grad_gate = (grad_hidden * up_pre * sigmoid_g * (1.0 + gate_pre * (1.0 - sigmoid_g))).astype(jnp.bfloat16)
    grad_aup = jnp.dot(lowrank.T, grad_gate, preferred_element_type=jnp.float32)
    grad_low = jnp.dot(grad_gate, adapter_up.T, preferred_element_type=jnp.float32).astype(jnp.bfloat16)
    grad_adown = jnp.dot(row_data.T, grad_low, preferred_element_type=jnp.float32)
    return grad_adown, grad_aup


def reference(tokens, grad_mixed, expert_ids, gate_probs, gate_proj, up_proj, down_proj, share_down, share_up, factor_down, factor_up):
    block_count = N_DP * N_EXPERT
    slot_count = TOK_DEV * TOP
    slot_maps, positions = jax.vmap(partial(slot_table, expert_count=EXPERTS, capacity=CAP))(expert_ids.reshape(block_count, TOK_DEV, TOP))
    by_expert = slot_maps.reshape(block_count, EXPERTS, CAP).transpose(1, 0, 2)
    offsets = jnp.arange(block_count, dtype=jnp.int32)[:, None] * slot_count
    sentinel = block_count * slot_count
    zero_row = jnp.zeros((1, D), tokens.dtype)
    tok_pad = jnp.concatenate([tokens, zero_row], axis=0)
    grad_pad = jnp.concatenate([grad_mixed, zero_row], axis=0)
    gate_pad = jnp.concatenate([gate_probs.reshape(-1), jnp.zeros((1,), gate_probs.dtype)])

    def per_expert(running, inputs):
        mixed_acc, share_acc_down, share_acc_up = running
        expert_slots, gate_mat, up_mat, down_mat, piece_down, piece_up = inputs
        global_slot = jnp.where(expert_slots < slot_count, expert_slots + offsets, sentinel).reshape(-1).astype(jnp.int32)
        token_idx = global_slot // TOP
        row_data = tok_pad[token_idx]
        adapter_down = expand(share_down, piece_down).astype(jnp.bfloat16)
        adapter_up = expand(share_up, piece_up).astype(jnp.bfloat16)
        result, lowrank, gate_pre, up_pre = expert_forward(row_data, gate_mat, up_mat, down_mat, adapter_down, adapter_up)
        weight_of = gate_pad[global_slot].astype(jnp.float32)
        mixed_acc = mixed_acc.at[token_idx].add(weight_of[:, None] * result.astype(jnp.float32))
        weighted = (weight_of[:, None] * grad_pad[token_idx].astype(jnp.float32)).astype(jnp.bfloat16)
        grad_adown, grad_aup = expert_backward(row_data, weighted, down_mat, adapter_up, lowrank, gate_pre, up_pre)
        bdown_grad, adown_grad = factor_grads(share_down, piece_down, grad_adown)
        bup_grad, aup_grad = factor_grads(share_up, piece_up, grad_aup)
        return (mixed_acc, share_acc_down + adown_grad, share_acc_up + aup_grad), (bdown_grad, bup_grad)

    initial = (jnp.zeros((TOKENS + 1, D), jnp.float32), jnp.zeros(share_down.shape, jnp.float32), jnp.zeros(share_up.shape, jnp.float32))
    finals, stacked = lax.scan(per_expert, initial, (by_expert, gate_proj, up_proj, down_proj, factor_down, factor_up))
    mixed_acc, adown_total, aup_total = finals
    bdown_all, bup_all = stacked
    return mixed_acc[:TOKENS].astype(jnp.bfloat16), bdown_all, bup_all, adown_total, aup_total
```

```python
import jax
import jax.numpy as jnp
from jax import lax
from jax.experimental import pallas as pl
from jax.experimental.pallas import tpu as pltpu
from jax.sharding import PartitionSpec as P


F32 = jnp.float32
BF16 = jnp.bfloat16
SIDE = 4
NT = (((1,), (1,)), ((), ()))
TN = (((0,), (0,)), ((), ()))
NN = (((1,), (0,)), ((), ()))


def dot(a, b, dims):
    return lax.dot_general(a, b, dims, preferred_element_type=F32)


def fetch(value, dy, dx, flip=False):
    perm = []
    for y in range(SIDE):
        for x in range(SIDE):
            for c in range(2):
                source = (((y + dy) % SIDE) * SIDE + (x + dx) % SIDE) * 2 + (c ^ int(flip))
                perm.append((source, (y * SIDE + x) * 2 + c))
    return lax.ppermute(value, "expert", perm)


def fetch_dp(value, shift):
    return lax.ppermute(value, "dp", [((z + shift) % SIDE, z) for z in range(SIDE)])


def step(axis, k):
    return (k, 0) if axis == "y" else (0, k)


def ring_near(own, axis, flip):
    return fetch(own, *step(axis, 1), flip), fetch(own, *step(axis, 3), flip)


def ring_far(near, axis):
    up, down = near
    half = up.shape[0] // 2
    return fetch(up[:half], *step(axis, 1)), fetch(down[half:], *step(axis, 3))


def first_phase(half_block, axis):
    own = fetch(half_block, 0, 0, True)
    near = ring_near(half_block, axis, True)
    far = ring_far(near, axis)
    return jnp.stack([own, near[0], jnp.concatenate(far, axis=0), near[1]])


def sum_ring(own, axis):
    one, two, three = (fetch(own, *step(axis, k)) for k in (1, 2, 3))
    return (own + two) + (one + three)


def sum_dp(own):
    one, two, three = (fetch_dp(own, k) for k in (1, 2, 3))
    return (own + two) + (one + three)


def scatter_axis(chunks, axis):
    total = chunks[0].astype(F32)
    for k in (1, 2, 3):
        total = total + fetch(chunks[k], *step(axis, (SIDE - k) % SIDE)).astype(F32)
    return total.astype(BF16)


def piece_copies(pieces, buf, sems):
    half = buf.shape[-1] // 2
    left, right = pl.ds(0, half), pl.ds(half, half)
    a0, a1, a2a, a2b, a3, b0, b1, b2a, b2b, b3 = pieces
    places = [
        (a0, buf.at[0, :, :, left]),
        (a1, buf.at[1, :, :, left]),
        (a2a, buf.at[2, 0:2, :, left]),
        (a2b, buf.at[2, 2:4, :, left]),
        (a3, buf.at[3, :, :, left]),
        (b0, buf.at[:, 0, :, right]),
        (b1, buf.at[:, 1, :, right]),
        (b2a, buf.at[0:2, 2, :, right]),
        (b2b, buf.at[2:4, 2, :, right]),
        (b3, buf.at[:, 3, :, right]),
    ]
    return [pltpu.make_async_copy(s, d, sems.at[i]) for i, (s, d) in enumerate(places)]


def slot_match(rows_ref, b, weighted):
    rows = rows_ref[b]
    slot = lax.broadcasted_iota(jnp.int32, (64, rows.shape[1]), 0).astype(F32)
    if weighted:
        picked = jnp.where(slot == rows[0:1], rows[2:3], jnp.where(slot == rows[1:2], rows[3:4], 0.0))
    else:
        picked = jnp.where((slot == rows[0:1]) | (slot == rows[1:2]), 1.0, 0.0)
    return picked.astype(BF16)


def gather_rows(rows_ref, buf, dest, weighted):
    def body(b, carry):
        picked = slot_match(rows_ref, b, weighted)
        out = dot(picked, buf[b // SIDE, b % SIDE], NN).astype(BF16)
        dest[0, b] = out[0:32]
        dest[1, b] = out[32:64]
        return carry

    lax.fori_loop(0, SIDE * SIDE, body, 0)


TILE = 8


def tile_rows(ref, e, m):
    part = ref[e, pl.ds(m * TILE, TILE)]
    return part.reshape(TILE * part.shape[1], part.shape[2])


def forward_kernel(*refs):
    pieces, (rows_ref, gate_h, up_h, down_h, adn_ref, aup_ref) = refs[:10], refs[10:16]
    part_h, rows_h, low_ref, act_h = refs[16:20]
    buf, gate_v, up_v, down_v, rows_v, res_v, act_v, sems, wsems, osems = refs[20:]
    loads = piece_copies(pieces, buf, sems)
    for c in loads:
        c.start()
    weights = []
    for e in range(2):
        weights.append(
            [
                pltpu.make_async_copy(gate_h.at[e], gate_v.at[e], wsems.at[e, 0]),
                pltpu.make_async_copy(up_h.at[e], up_v.at[e], wsems.at[e, 1]),
                pltpu.make_async_copy(down_h.at[e], down_v.at[e], wsems.at[e, 2]),
            ]
        )
        for c in weights[e]:
            c.start()
    for c in loads:
        c.wait()
    gather_rows(rows_ref, buf, rows_v, False)
    save_rows = pltpu.make_async_copy(rows_v, rows_h, osems.at[0])
    save_rows.start()
    saves = [save_rows]
    for e in range(2):
        for c in weights[e]:
            c.wait()

        def body(m, carry, e=e):
            data = tile_rows(rows_v, e, m)
            low = dot(data, adn_ref[e], NT).astype(BF16)
            low_ref[e, m] = low
            gate = dot(data, gate_v[e], NN) + dot(low, aup_ref[e], NN)
            up = dot(data, up_v[e], NN)
            sig = 1.0 / (1.0 + jnp.exp(-gate))
            hidden = (gate * sig * up).astype(BF16)
            act_v[e, m] = up * sig * (1.0 + gate * (1.0 - sig))
            res = dot(hidden, down_v[e], NN).astype(BF16)
            res_v[e, pl.ds(m * TILE, TILE)] = res.reshape(TILE, 32, res.shape[1])
            return carry

        lax.fori_loop(0, SIDE * SIDE // TILE, body, 0)
        save_act = pltpu.make_async_copy(act_v.at[e], act_h.at[e], osems.at[1 + e])
        save_act.start()
        saves.append(save_act)
    for dy in range(SIDE):

        def mix(dx, carry, dy=dy):
            b = dy * SIDE + dx
            picked = slot_match(rows_ref, b, True)
            both = jnp.concatenate([res_v[0, b], res_v[1, b]], axis=0)
            buf[dy, dx] = dot(picked, both, TN).astype(BF16)
            return carry

        lax.fori_loop(0, SIDE, mix, 0)
        save = pltpu.make_async_copy(buf.at[dy], part_h.at[dy], osems.at[3 + dy])
        save.start()
        saves.append(save)
    for c in saves:
        c.wait()


def forward_call(pieces, rows, gate, up, down, adn, aup):
    tok, width = pieces[0].shape[1], 2 * pieces[0].shape[2]
    ff, rank = gate.shape[2], adn.shape[1]
    any_spec = pl.BlockSpec(memory_space=pl.ANY)
    vmem = pl.BlockSpec(memory_space=pltpu.VMEM)
    nb = SIDE * SIDE
    tiles, tile = nb // TILE, TILE * 32
    return pl.pallas_call(
        forward_kernel,
        out_shape=(
            jax.ShapeDtypeStruct((SIDE, SIDE, tok, width), BF16),
            jax.ShapeDtypeStruct((2, nb, 32, width), BF16),
            jax.ShapeDtypeStruct((2, tiles, tile, rank), BF16),
            jax.ShapeDtypeStruct((2, tiles, tile, ff), F32),
        ),
        in_specs=[any_spec] * 10 + [vmem] + [any_spec] * 3 + [vmem] * 2,
        out_specs=(any_spec, any_spec, vmem, any_spec),
        scratch_shapes=[
            pltpu.VMEM((SIDE, SIDE, tok, width), BF16),
            pltpu.VMEM((2, width, ff), BF16),
            pltpu.VMEM((2, width, ff), BF16),
            pltpu.VMEM((2, ff, width), BF16),
            pltpu.VMEM((2, nb, 32, width), BF16),
            pltpu.VMEM((2, nb, 32, width), BF16),
            pltpu.VMEM((2, tiles, tile, ff), F32),
            pltpu.SemaphoreType.DMA((10,)),
            pltpu.SemaphoreType.DMA((2, 3)),
            pltpu.SemaphoreType.DMA((7,)),
        ],
        compiler_params=pltpu.CompilerParams(vmem_limit_bytes=60 * 1024 * 1024),
        cost_estimate=pl.CostEstimate(
            flops=2 * nb * 64 * width * (3 * ff + 256), transcendentals=nb * 64 * ff, bytes_accessed=50_000_000
        ),
        name="expert_forward",
    )(*pieces, rows, gate, up, down, adn, aup)


def backward_kernel(final, *refs):
    pieces, (rows_ref, down_h, aup_ref, rows_h, low_ref, act_h) = refs[:10], refs[10:16]
    rest = refs[16:]
    if final:
        adn0_ref, aup0_ref, sd_ref, fdt_ref, sx_ref, fut_ref = rest[:6]
        gfd_ref, gfu_ref, gsd_ref, gsu_ref = rest[6:10]
        gadn, gaup, rest = rest[10], rest[11], rest[12:]
    else:
        gadn, gaup, rest = rest[0], rest[1], rest[2:]
    buf, down_v, rows_v, grad_v, act_v, sems, wsems = rest
    loads = piece_copies(pieces, buf, sems)
    for c in loads:
        c.start()
    more = []
    for e in range(2):
        more.append(
            [
                pltpu.make_async_copy(down_h.at[e], down_v.at[e], wsems.at[e, 0]),
                pltpu.make_async_copy(act_h.at[e], act_v.at[e], wsems.at[e, 1]),
                pltpu.make_async_copy(rows_h.at[e], rows_v.at[e], wsems.at[e, 2]),
            ]
        )
        for c in more[e]:
            c.start()
    if final:
        gadn[...] = adn0_ref[...]
        gaup[...] = aup0_ref[...]
    else:
        gadn[...] = jnp.zeros(gadn.shape, F32)
        gaup[...] = jnp.zeros(gaup.shape, F32)
    for c in loads:
        c.wait()
    gather_rows(rows_ref, buf, grad_v, True)
    for e in range(2):
        for c in more[e]:
            c.wait()

        def body(m, carry, e=e):
            weighted = tile_rows(grad_v, e, m)
            data = tile_rows(rows_v, e, m)
            grad_hidden = dot(weighted, down_v[e], NT)
            grad_gate = (grad_hidden * act_v[e, m]).astype(BF16)
            grad_low = dot(grad_gate, aup_ref[e], NT).astype(BF16)
            gaup[e] += dot(low_ref[e, m], grad_gate, TN)
            gadn[e] += dot(grad_low, data, TN)
            return carry

        lax.fori_loop(0, SIDE * SIDE // TILE, body, 0)
    if not final:
        return
    kron = fdt_ref.shape[1]
    dn, up = fdt_ref.shape[2], fut_ref.shape[2]
    wide, quarter = fdt_ref.shape[3], fut_ref.shape[3] // kron
    gsd_ref[...] = jnp.zeros(gsd_ref.shape, F32)
    gsu_ref[...] = jnp.zeros(gsu_ref.shape, F32)
    for e in range(2):
        for i in range(kron):
            factor = fdt_ref[e, i]
            total = jnp.zeros((dn, wide), F32)
            for a in range(kron):
                for c in range(kron):
                    block = gadn[e, c * dn : (c + 1) * dn, a * wide : (a + 1) * wide]
                    place = (i * kron + a) * kron + c
                    total = total + sd_ref[place] * block
                    line = jnp.sum(factor * block, axis=0, keepdims=True)
                    short = line[:, 0:128]
                    for w in range(128, wide, 128):
                        short = short + line[:, w : w + 128]
                    gsd_ref[place : place + 1] += short
            gfd_ref[e, i] = total
            factor = fut_ref[e, i]
            total = jnp.zeros(factor.shape, F32)
            for a in range(kron):
                block = gaup[e, a * up : (a + 1) * up]
                place = i * kron + a
                total = total + sx_ref[place : place + 1] * block
                gsu_ref[place : place + 1] += jnp.sum(factor * block, axis=0, keepdims=True)
            folded = total[:, 0:quarter]
            for c in range(1, kron):
                folded = folded + total[:, c * quarter : (c + 1) * quarter]
            gfu_ref[e, i] = folded


def backward_call(pieces, rows, down, aup, stash, tail=None):
    tok, width = pieces[0].shape[1], 2 * pieces[0].shape[2]
    ff, rank = down.shape[1], aup.shape[1]
    any_spec = pl.BlockSpec(memory_space=pl.ANY)
    vmem = pl.BlockSpec(memory_space=pltpu.VMEM)
    nb = SIDE * SIDE
    tiles, tile = nb // TILE, TILE * 32
    saved_rows, saved_low, saved_act = stash
    args = [*pieces, rows, down, aup, saved_rows, saved_low, saved_act]
    in_specs = [any_spec] * 10 + [vmem, any_spec, vmem, any_spec, vmem, any_spec]
    sums = [(2, rank, width), (2, rank, ff)]
    scratch = []
    if tail is None:
        out_shape = tuple(jax.ShapeDtypeStruct(s, F32) for s in sums)
    else:
        (adn0, aup0), share_down, fdt, sx, fut = tail
        kron = fdt.shape[1]
        args += [adn0, aup0, share_down.reshape(-1), fdt, sx, fut]
        in_specs += [vmem, vmem, pl.BlockSpec(memory_space=pltpu.SMEM), vmem, vmem, vmem]
        out_shape = (
            jax.ShapeDtypeStruct(fdt.shape, F32),
            jax.ShapeDtypeStruct(fut.shape[:3] + (ff // kron,), F32),
            jax.ShapeDtypeStruct((kron**3, 128), F32),
            jax.ShapeDtypeStruct((kron**2, ff), F32),
        )
        scratch = [pltpu.VMEM(s, F32) for s in sums]
    return pl.pallas_call(
        lambda *refs: backward_kernel(tail is not None, *refs),
        out_shape=out_shape,
        in_specs=in_specs,
        out_specs=tuple(vmem for _ in out_shape),
        scratch_shapes=scratch
        + [
            pltpu.VMEM((SIDE, SIDE, tok, width), BF16),
            pltpu.VMEM((2, ff, width), BF16),
            pltpu.VMEM((2, nb, 32, width), BF16),
            pltpu.VMEM((2, nb, 32, width), BF16),
            pltpu.VMEM((2, tiles, tile, ff), F32),
            pltpu.SemaphoreType.DMA((10,)),
            pltpu.SemaphoreType.DMA((2, 3)),
        ],
        compiler_params=pltpu.CompilerParams(vmem_limit_bytes=60 * 1024 * 1024),
        cost_estimate=pl.CostEstimate(
            flops=2 * nb * 64 * width * (ff + 256), transcendentals=0, bytes_accessed=30_000_000
        ),
        name="expert_backward" if tail is None else "expert_backward_last",
    )(*args)


def routing_rows(info, first_expert):
    ids, probs = info[:, 0:8].astype(F32), info[:, 8:16].astype(F32)
    tok = info.shape[2]
    earlier = (jnp.arange(tok)[:, None] < jnp.arange(tok)[None, :]).astype(BF16)
    slots, weights = [], []
    for e in range(2):
        hit = ids == (first_expert + e).astype(F32)
        routed = jnp.any(hit, axis=1)
        before = jnp.dot(routed.astype(BF16), earlier, preferred_element_type=F32)
        slots.append(jnp.where(routed, before + 32.0 * e, -1.0))
        weights.append(jnp.sum(jnp.where(hit, probs, 0.0), axis=1))
    zero = jnp.zeros_like(slots[0])
    return jnp.stack([*slots, *weights, zero, zero, zero, zero], axis=1)


def gather_small(info):
    def spread(own, axis, flip):
        return jnp.concatenate([fetch(own, *step(axis, k), flip) for k in range(1, 4)], axis=0)

    row = jnp.concatenate([fetch(info, 0, 0, True), spread(info, "x", True)], axis=0)
    cross = jnp.concatenate([row, spread(row, "y", False)], axis=0)
    return cross, fetch(cross, 0, 0, True)


def on_device(
    tokens,
    grad_mixed,
    expert_ids,
    gate_probs,
    gate_proj,
    up_proj,
    down_proj,
    share_down,
    share_up,
    factor_down,
    factor_up,
):
    width = tokens.shape[1]
    half = width // 2
    kron = share_down.shape[0]
    local = gate_proj.shape[0]
    ff = gate_proj.shape[2]
    first_expert = lax.axis_index("expert") * local

    info = jnp.concatenate([expert_ids.T.astype(BF16), gate_probs.T], axis=0)[None]
    info_cross, info_own = gather_small(info)
    rows_cross = routing_rows(info_cross, first_expert)
    rows_own = routing_rows(info_own, first_expert)

    highest = lax.Precision.HIGHEST
    adn = jnp.einsum("iac,eibd->ecdab", share_down, factor_down, precision=highest)
    adn = adn.reshape(local, -1, width).astype(BF16)
    aup = jnp.einsum("iac,eibd->eabcd", share_up, factor_up, precision=highest)
    aup = aup.reshape(local, -1, ff).astype(BF16)
    fdt = factor_down.transpose(0, 1, 3, 2)
    fut = jnp.tile(factor_up, (1, 1, 1, kron))
    sx = jnp.repeat(share_up, ff // kron, axis=2).reshape(kron * kron, ff)

    tok_a = first_phase(tokens[:, :half], "x")
    tok_b = first_phase(tokens[:, half:], "y")
    grad_a = first_phase(grad_mixed[:, :half], "x")
    grad_b = first_phase(grad_mixed[:, half:], "y")

    def second_phase(left, right):
        near_a, near_b = ring_near(left, "y", False), ring_near(right, "x", False)
        return near_a, near_b

    def all_pieces(left, right, near_a, near_b):
        far_a, far_b = ring_far(near_a, "y"), ring_far(near_b, "x")
        return [left, near_a[0], *far_a, near_a[1], right, near_b[0], *far_b, near_b[1]]

    near_ta, near_tb = second_phase(tok_a, tok_b)
    grad_a, grad_b, near_ta, near_tb = lax.optimization_barrier((grad_a, grad_b, near_ta, near_tb))
    tok_cross = all_pieces(tok_a, tok_b, near_ta, near_tb)
    tok_own = [fetch(p, 0, 0, True) for p in tok_cross]
    near_ga, near_gb = second_phase(grad_a, grad_b)
    grad_cross = all_pieces(grad_a, grad_b, near_ga, near_gb)
    grad_own = [fetch(p, 0, 0, True) for p in grad_cross]

    part_cross, *stash_cross = forward_call(tok_cross, rows_cross, gate_proj, up_proj, down_proj, adn, aup)
    part_back = fetch(part_cross, 0, 0, True)
    part_own, *stash_own = forward_call(tok_own, rows_own, gate_proj, up_proj, down_proj, adn, aup)

    def both(cut):
        return (cut(part_own).astype(F32) + cut(part_back).astype(F32)).astype(BF16)

    out_a = scatter_axis([both(lambda p, k=k: p[k, :, :, :half]) for k in range(SIDE)], "y")
    out_b = scatter_axis([both(lambda p, k=k: p[:, k, :, half:]) for k in range(SIDE)], "x")
    out_a = scatter_axis([out_a[k] for k in range(SIDE)], "x")
    out_b = scatter_axis([out_b[k] for k in range(SIDE)], "y")
    mixed = jnp.concatenate([out_a, out_b], axis=1)

    sums = backward_call(grad_cross, rows_cross, down_proj, aup, stash_cross)
    gfd, gfu, gsd, gsu = backward_call(
        grad_own, rows_own, down_proj, aup, stash_own, (sums, share_down, fdt, sx, fut)
    )
    gsd = jnp.sum(gsd, axis=1)
    gsu = jnp.sum(gsu.reshape(kron**3, ff // kron), axis=1)
    shares = jnp.concatenate([gsd, gsu]).reshape(1, -1)
    shares = sum_dp(shares)
    shares = sum_ring(shares, "x")
    shares = sum_ring(shares, "y")
    shares = shares + fetch(shares, 0, 0, True)
    gfd, gfu = sum_dp(gfd), sum_dp(gfu)
    shares = shares.reshape(2, kron, kron, kron)
    return (mixed, gfd.transpose(0, 1, 3, 2), gfu, shares[0], shares[1])


def solution(mesh):
    return jax.shard_map(
        on_device,
        mesh=mesh,
        in_specs=(
            P(("dp", "expert"), None),
            P(("dp", "expert"), None),
            P(("dp", "expert"), None),
            P(("dp", "expert"), None),
            P("expert", None, None),
            P("expert", None, None),
            P("expert", None, None),
            P(),
            P(),
            P("expert", None, None, None),
            P("expert", None, None, None),
        ),
        out_specs=(
            P(("dp", "expert"), None),
            P("expert", None, None, None),
            P("expert", None, None, None),
            P(),
            P(),
        ),
        check_vma=False,
    )
```

```python
import jax
import jax.numpy as jnp
from jax import lax
from jax.experimental import pallas as pl
from jax.experimental.pallas import tpu as pltpu
from jax.sharding import PartitionSpec as P


F32 = jnp.float32
BF16 = jnp.bfloat16
SIDE = 4
NT = (((1,), (1,)), ((), ()))
TN = (((0,), (0,)), ((), ()))
NN = (((1,), (0,)), ((), ()))


def dot(a, b, dims):
    return lax.dot_general(a, b, dims, preferred_element_type=F32)


def fetch(value, dy, dx, flip=False):
    perm = []
    for y in range(SIDE):
        for x in range(SIDE):
            for c in range(2):
                source = (((y + dy) % SIDE) * SIDE + (x + dx) % SIDE) * 2 + (c ^ int(flip))
                perm.append((source, (y * SIDE + x) * 2 + c))
    return lax.ppermute(value, "expert", perm)


def fetch_dp(value, shift):
    return lax.ppermute(value, "dp", [((z + shift) % SIDE, z) for z in range(SIDE)])


def step(axis, k):
    return (k, 0) if axis == "y" else (0, k)


def ring_others(own, axis, flip=False):
    return [fetch(own, *step(axis, k), flip) for k in (1, 2, 3)]


def sum_pairs(value):
    for bit in (1, 2, 4, 8, 16):
        value = value + lax.ppermute(value, "expert", [(i ^ bit, i) for i in range(2 * SIDE * SIDE)])
    return value


def sum_dp(own):
    one, two, three = (fetch_dp(own, k) for k in (1, 2, 3))
    return (own + two) + (one + three)


def scatter_axis(chunks, axis):
    total = chunks[0].astype(F32)
    for k in (1, 2, 3):
        total = total + fetch(chunks[k], *step(axis, (SIDE - k) % SIDE)).astype(F32)
    return total.astype(BF16)


def piece_copies(pieces, buf, sems):
    tok, half = buf.shape[2], buf.shape[3] // 2
    left, right = pl.ds(0, half), pl.ds(half, half)
    places = [(p, buf.at[k, :, :, left]) for k, p in enumerate(pieces[:SIDE])]
    places += [(p, buf.at[:, k, :, right]) for k, p in enumerate(pieces[SIDE:])]
    return [pltpu.make_async_copy(s.at[:, 0:tok], d, sems.at[i]) for i, (s, d) in enumerate(places)]


def slot_match(rows_ref, b, weighted):
    rows = rows_ref[b]
    slot = lax.broadcasted_iota(jnp.int32, (64, rows.shape[1]), 0).astype(F32)
    if weighted:
        picked = jnp.where(slot == rows[0:1], rows[2:3], jnp.where(slot == rows[1:2], rows[3:4], 0.0))
    else:
        picked = jnp.where((slot == rows[0:1]) | (slot == rows[1:2]), 1.0, 0.0)
    return picked.astype(BF16)


def gather_rows(rows_ref, buf, dest, weighted):
    def body(b, carry):
        picked = slot_match(rows_ref, b, weighted)
        out = dot(picked, buf[b // SIDE, b % SIDE], NN).astype(BF16)
        dest[0, b] = out[0:32]
        dest[1, b] = out[32:64]
        return carry

    lax.fori_loop(0, SIDE * SIDE, body, 0)


TILE = 8


def tile_rows(ref, e, m):
    part = ref[e, pl.ds(m * TILE, TILE)]
    return part.reshape(TILE * part.shape[1], part.shape[2])


def forward_kernel(*refs):
    pieces, (rows_ref, gate_h, up_h, down_h, adn_ref, aup_ref) = refs[:8], refs[8:14]
    part_h, rows_h, low_ref, act_h = refs[14:18]
    buf, gate_v, up_v, down_v, rows_v, res_v, act_v, sems, wsems, osems = refs[18:]
    loads = piece_copies(pieces, buf, sems)
    for c in loads:
        c.start()
    weights = []
    for e in range(2):
        weights.append(
            [
                pltpu.make_async_copy(gate_h.at[e], gate_v.at[e], wsems.at[e, 0]),
                pltpu.make_async_copy(up_h.at[e], up_v.at[e], wsems.at[e, 1]),
                pltpu.make_async_copy(down_h.at[e], down_v.at[e], wsems.at[e, 2]),
            ]
        )
        for c in weights[e]:
            c.start()
    for c in loads:
        c.wait()
    gather_rows(rows_ref, buf, rows_v, False)
    save_rows = pltpu.make_async_copy(rows_v, rows_h, osems.at[0])
    save_rows.start()
    saves = [save_rows]
    for e in range(2):
        for c in weights[e]:
            c.wait()

        def body(m, carry, e=e):
            data = tile_rows(rows_v, e, m)
            low = dot(data, adn_ref[e], NT).astype(BF16)
            low_ref[e, m] = low
            gate = dot(data, gate_v[e], NN) + dot(low, aup_ref[e], NN)
            up = dot(data, up_v[e], NN)
            sig = 1.0 / (1.0 + jnp.exp(-gate))
            hidden = (gate * sig * up).astype(BF16)
            act_v[e, m] = up * sig * (1.0 + gate * (1.0 - sig))
            res = dot(hidden, down_v[e], NN).astype(BF16)
            res_v[e, pl.ds(m * TILE, TILE)] = res.reshape(TILE, 32, res.shape[1])
            return carry

        lax.fori_loop(0, SIDE * SIDE // TILE, body, 0)
        save_act = pltpu.make_async_copy(act_v.at[e], act_h.at[e], osems.at[1 + e])
        save_act.start()
        saves.append(save_act)
    for dy in range(SIDE):

        def mix(dx, carry, dy=dy):
            b = dy * SIDE + dx
            picked = slot_match(rows_ref, b, True)
            both = jnp.concatenate([res_v[0, b], res_v[1, b]], axis=0)
            buf[dy, dx] = dot(picked, both, TN).astype(BF16)
            return carry

        lax.fori_loop(0, SIDE, mix, 0)
        save = pltpu.make_async_copy(buf.at[dy], part_h.at[dy], osems.at[3 + dy])
        save.start()
        saves.append(save)
    for c in saves:
        c.wait()


def forward_call(pieces, rows, gate, up, down, adn, aup):
    tok, width = rows.shape[2], 2 * pieces[0].shape[2]
    ff, rank = gate.shape[2], adn.shape[1]
    any_spec = pl.BlockSpec(memory_space=pl.ANY)
    vmem = pl.BlockSpec(memory_space=pltpu.VMEM)
    nb = SIDE * SIDE
    tiles, tile = nb // TILE, TILE * 32
    return pl.pallas_call(
        forward_kernel,
        out_shape=(
            jax.ShapeDtypeStruct((SIDE, SIDE, tok, width), BF16),
            jax.ShapeDtypeStruct((2, nb, 32, width), BF16),
            jax.ShapeDtypeStruct((2, tiles, tile, rank), BF16),
            jax.ShapeDtypeStruct((2, tiles, tile, ff), F32),
        ),
        in_specs=[any_spec] * 8 + [vmem] + [any_spec] * 3 + [vmem] * 2,
        out_specs=(any_spec, any_spec, vmem, any_spec),
        scratch_shapes=[
            pltpu.VMEM((SIDE, SIDE, tok, width), BF16),
            pltpu.VMEM((2, width, ff), BF16),
            pltpu.VMEM((2, width, ff), BF16),
            pltpu.VMEM((2, ff, width), BF16),
            pltpu.VMEM((2, nb, 32, width), BF16),
            pltpu.VMEM((2, nb, 32, width), BF16),
            pltpu.VMEM((2, tiles, tile, ff), F32),
            pltpu.SemaphoreType.DMA((8,)),
            pltpu.SemaphoreType.DMA((2, 3)),
            pltpu.SemaphoreType.DMA((7,)),
        ],
        compiler_params=pltpu.CompilerParams(vmem_limit_bytes=60 * 1024 * 1024),
        cost_estimate=pl.CostEstimate(
            flops=2 * nb * 64 * width * (3 * ff + 256), transcendentals=nb * 64 * ff, bytes_accessed=50_000_000
        ),
        name="expert_forward",
    )(*pieces, rows, gate, up, down, adn, aup)


def backward_kernel(final, *refs):
    pieces, (rows_ref, down_h, aup_ref, rows_h, low_ref, act_h) = refs[:8], refs[8:14]
    rest = refs[14:]
    if final:
        adn0_ref, aup0_ref, sd_ref, fdt_ref, sx_ref, fut_ref = rest[:6]
        gfd_ref, gfu_ref, gsd_ref, gsu_ref = rest[6:10]
        gadn, gaup, rest = rest[10], rest[11], rest[12:]
    else:
        gadn, gaup, rest = rest[0], rest[1], rest[2:]
    buf, down_v, rows_v, grad_v, act_v, sems, wsems = rest
    loads = piece_copies(pieces, buf, sems)
    for c in loads:
        c.start()
    more = []
    for e in range(2):
        more.append(
            [
                pltpu.make_async_copy(down_h.at[e], down_v.at[e], wsems.at[e, 0]),
                pltpu.make_async_copy(act_h.at[e], act_v.at[e], wsems.at[e, 1]),
                pltpu.make_async_copy(rows_h.at[e], rows_v.at[e], wsems.at[e, 2]),
            ]
        )
        for c in more[e]:
            c.start()
    if final:
        gadn[...] = adn0_ref[...]
        gaup[...] = aup0_ref[...]
    else:
        gadn[...] = jnp.zeros(gadn.shape, F32)
        gaup[...] = jnp.zeros(gaup.shape, F32)
    for c in loads:
        c.wait()
    gather_rows(rows_ref, buf, grad_v, True)
    for e in range(2):
        for c in more[e]:
            c.wait()

        def body(m, carry, e=e):
            weighted = tile_rows(grad_v, e, m)
            data = tile_rows(rows_v, e, m)
            grad_hidden = dot(weighted, down_v[e], NT)
            grad_gate = (grad_hidden * act_v[e, m]).astype(BF16)
            grad_low = dot(grad_gate, aup_ref[e], NT).astype(BF16)
            gaup[e] += dot(low_ref[e, m], grad_gate, TN)
            gadn[e] += dot(grad_low, data, TN)
            return carry

        lax.fori_loop(0, SIDE * SIDE // TILE, body, 0)
    if not final:
        return
    kron = fdt_ref.shape[1]
    dn, up = fdt_ref.shape[2], fut_ref.shape[2]
    wide, quarter = fdt_ref.shape[3], fut_ref.shape[3] // kron
    gsd_ref[...] = jnp.zeros(gsd_ref.shape, F32)
    gsu_ref[...] = jnp.zeros(gsu_ref.shape, F32)
    for e in range(2):
        for i in range(kron):
            factor = fdt_ref[e, i]
            total = jnp.zeros((dn, wide), F32)
            for a in range(kron):
                for c in range(kron):
                    block = gadn[e, c * dn : (c + 1) * dn, a * wide : (a + 1) * wide]
                    place = (i * kron + a) * kron + c
                    total = total + sd_ref[place] * block
                    line = jnp.sum(factor * block, axis=0, keepdims=True)
                    short = line[:, 0:128]
                    for w in range(128, wide, 128):
                        short = short + line[:, w : w + 128]
                    gsd_ref[place : place + 1] += short
            gfd_ref[e, i] = total
            factor = fut_ref[e, i]
            total = jnp.zeros(factor.shape, F32)
            for a in range(kron):
                block = gaup[e, a * up : (a + 1) * up]
                place = i * kron + a
                total = total + sx_ref[place : place + 1] * block
                gsu_ref[place : place + 1] += jnp.sum(factor * block, axis=0, keepdims=True)
            folded = total[:, 0:quarter]
            for c in range(1, kron):
                folded = folded + total[:, c * quarter : (c + 1) * quarter]
            gfu_ref[e, i] = folded


def backward_call(pieces, rows, down, aup, stash, tail=None):
    tok, width = pieces[0].shape[1], 2 * pieces[0].shape[2]
    ff, rank = down.shape[1], aup.shape[1]
    any_spec = pl.BlockSpec(memory_space=pl.ANY)
    vmem = pl.BlockSpec(memory_space=pltpu.VMEM)
    nb = SIDE * SIDE
    tiles, tile = nb // TILE, TILE * 32
    saved_rows, saved_low, saved_act = stash
    args = [*pieces, rows, down, aup, saved_rows, saved_low, saved_act]
    in_specs = [any_spec] * 8 + [vmem, any_spec, vmem, any_spec, vmem, any_spec]
    sums = [(2, rank, width), (2, rank, ff)]
    scratch = []
    if tail is None:
        out_shape = tuple(jax.ShapeDtypeStruct(s, F32) for s in sums)
    else:
        (adn0, aup0), share_down, fdt, sx, fut = tail
        kron = fdt.shape[1]
        args += [adn0, aup0, share_down.reshape(-1), fdt, sx, fut]
        in_specs += [vmem, vmem, pl.BlockSpec(memory_space=pltpu.SMEM), vmem, vmem, vmem]
        out_shape = (
            jax.ShapeDtypeStruct(fdt.shape, F32),
            jax.ShapeDtypeStruct(fut.shape[:3] + (ff // kron,), F32),
            jax.ShapeDtypeStruct((kron**3, 128), F32),
            jax.ShapeDtypeStruct((kron**2, ff), F32),
        )
        scratch = [pltpu.VMEM(s, F32) for s in sums]
    return pl.pallas_call(
        lambda *refs: backward_kernel(tail is not None, *refs),
        out_shape=out_shape,
        in_specs=in_specs,
        out_specs=tuple(vmem for _ in out_shape),
        scratch_shapes=scratch
        + [
            pltpu.VMEM((SIDE, SIDE, tok, width), BF16),
            pltpu.VMEM((2, ff, width), BF16),
            pltpu.VMEM((2, nb, 32, width), BF16),
            pltpu.VMEM((2, nb, 32, width), BF16),
            pltpu.VMEM((2, tiles, tile, ff), F32),
            pltpu.SemaphoreType.DMA((8,)),
            pltpu.SemaphoreType.DMA((2, 3)),
        ],
        compiler_params=pltpu.CompilerParams(vmem_limit_bytes=60 * 1024 * 1024),
        cost_estimate=pl.CostEstimate(
            flops=2 * nb * 64 * width * (ff + 256), transcendentals=0, bytes_accessed=30_000_000
        ),
        name="expert_backward" if tail is None else "expert_backward_last",
    )(*args)


def routing_rows(pieces, first_expert, tok):
    ids = jnp.stack([p[:, tok] for p in pieces[:SIDE]], axis=0)
    probs = jnp.stack([p[:, tok] for p in pieces[SIDE:]], axis=1)
    ids, probs = (v.astype(F32).reshape(SIDE * SIDE, -1, tok) for v in (ids, probs))
    earlier = (jnp.arange(tok)[:, None] < jnp.arange(tok)[None, :]).astype(BF16)
    slots, weights = [], []
    for e in range(2):
        hit = ids == (first_expert + e).astype(F32)
        routed = jnp.any(hit, axis=1)
        before = jnp.dot(routed.astype(BF16), earlier, preferred_element_type=F32)
        slots.append(jnp.where(routed, before + 32.0 * e, -1.0))
        weights.append(jnp.sum(jnp.where(hit, probs, 0.0), axis=1))
    zero = jnp.zeros_like(slots[0])
    return jnp.stack([*slots, *weights, zero, zero, zero, zero], axis=1)


def layer(
    tokens,
    grad_mixed,
    expert_ids,
    gate_probs,
    gate_proj,
    up_proj,
    down_proj,
    share_down,
    share_up,
    factor_down,
    factor_up,
):
    tok, width = tokens.shape
    half = width // 2
    kron = share_down.shape[0]
    local = gate_proj.shape[0]
    ff = gate_proj.shape[2]
    first_expert = lax.axis_index("expert") * local

    highest = lax.Precision.HIGHEST
    adn = jnp.einsum("iac,eibd->ecdab", share_down, factor_down, precision=highest)
    adn = adn.reshape(local, -1, width).astype(BF16)
    aup = jnp.einsum("iac,eibd->eabcd", share_up, factor_up, precision=highest)
    aup = aup.reshape(local, -1, ff).astype(BF16)
    fdt = factor_down.transpose(0, 1, 3, 2)
    fut = jnp.tile(factor_up, (1, 1, 1, kron))
    sx = jnp.repeat(share_up, ff // kron, axis=2).reshape(kron * kron, ff)

    info = jnp.concatenate([expert_ids.T.astype(BF16), gate_probs.T], axis=0).reshape(1, width)
    block = jnp.concatenate([grad_mixed, tokens, jnp.pad(info, ((0, 7), (0, 0)))], axis=0)
    own = fetch(block, 0, 0, True)
    left = [own[:, :half], *ring_others(block[:, :half], "x", True)]
    right = [own[:, half:], *ring_others(block[:, half:], "y", True)]
    tok_left, tok_right = (jnp.stack([v[tok:] for v in side]) for side in (left, right))
    grad_left, grad_right = (jnp.stack([v[:tok] for v in side]) for side in (left, right))

    tok_cross = [tok_left, *ring_others(tok_left, "y"), tok_right, *ring_others(tok_right, "x")]
    tied = lax.optimization_barrier((grad_left, grad_right, *tok_cross))
    (grad_left, grad_right), tok_cross = tied[:2], list(tied[2:])
    tok_own = [fetch(p, 0, 0, True) for p in tok_cross]
    grad_cross = [grad_left, *ring_others(grad_left, "y"), grad_right, *ring_others(grad_right, "x")]
    grad_own = [fetch(p, 0, 0, True) for p in grad_cross]
    rows_cross = routing_rows(tok_cross, first_expert, tok)
    rows_own = routing_rows(tok_own, first_expert, tok)

    part_cross, *stash_cross = forward_call(tok_cross, rows_cross, gate_proj, up_proj, down_proj, adn, aup)
    part_back = fetch(part_cross, 0, 0, True)
    part_own, *stash_own = forward_call(tok_own, rows_own, gate_proj, up_proj, down_proj, adn, aup)

    def both(cut):
        return (cut(part_own).astype(F32) + cut(part_back).astype(F32)).astype(BF16)

    out_a = scatter_axis([both(lambda p, k=k: p[k, :, :, :half]) for k in range(SIDE)], "y")
    out_b = scatter_axis([both(lambda p, k=k: p[:, k, :, half:]) for k in range(SIDE)], "x")
    out_a = scatter_axis([out_a[k] for k in range(SIDE)], "x")
    out_b = scatter_axis([out_b[k] for k in range(SIDE)], "y")
    mixed = jnp.concatenate([out_a, out_b], axis=1)

    sums = backward_call(grad_cross, rows_cross, down_proj, aup, stash_cross)
    gfd, gfu, gsd, gsu = backward_call(
        grad_own, rows_own, down_proj, aup, stash_own, (sums, share_down, fdt, sx, fut)
    )
    gsd = jnp.sum(gsd, axis=1)
    gsu = jnp.sum(gsu.reshape(kron**3, ff // kron), axis=1)
    shares = jnp.concatenate([gsd, gsu]).reshape(1, -1)
    shape_fd, shape_fu = gfd.shape, gfu.shape
    packed = jnp.concatenate([gfd.reshape(-1, 128), gfu.reshape(-1, 128), shares], axis=0)
    packed = sum_dp(packed)
    cut = gfd.size // 128
    gfd = packed[:cut].reshape(shape_fd)
    gfu = packed[cut:-1].reshape(shape_fu)
    shares = sum_pairs(packed[-1:])
    shares = shares.reshape(2, kron, kron, kron)
    return (mixed, gfd.transpose(0, 1, 3, 2), gfu, shares[0], shares[1])


def solution(mesh):
    step = shard_map_step(mesh)
    return step


def shard_map_step(mesh):
    return jax.shard_map(
        layer,
        mesh=mesh,
        in_specs=(
            P(("dp", "expert"), None),
            P(("dp", "expert"), None),
            P(("dp", "expert"), None),
            P(("dp", "expert"), None),
            P("expert", None, None),
            P("expert", None, None),
            P("expert", None, None),
            P(),
            P(),
            P("expert", None, None, None),
            P("expert", None, None, None),
        ),
        out_specs=(
            P(("dp", "expert"), None),
            P("expert", None, None, None),
            P("expert", None, None, None),
            P(),
            P(),
        ),
        check_vma=False,
    )
```

```python
import jax
import jax.numpy as jnp
from jax import lax
from jax.experimental import pallas as pl
from jax.experimental.pallas import tpu as pltpu
from jax.sharding import PartitionSpec as P


F32 = jnp.float32
BF16 = jnp.bfloat16
SIDE = 4
NT = (((1,), (1,)), ((), ()))
TN = (((0,), (0,)), ((), ()))
NN = (((1,), (0,)), ((), ()))


def dot(a, b, dims):
    return lax.dot_general(a, b, dims, preferred_element_type=F32)


def fetch(value, dy, dx, flip=False):
    perm = []
    for y in range(SIDE):
        for x in range(SIDE):
            for c in range(2):
                source = (((y + dy) % SIDE) * SIDE + (x + dx) % SIDE) * 2 + (c ^ int(flip))
                perm.append((source, (y * SIDE + x) * 2 + c))
    return lax.ppermute(value, "expert", perm)


def fetch_dp(value, shift):
    return lax.ppermute(value, "dp", [((z + shift) % SIDE, z) for z in range(SIDE)])


def step(axis, k):
    return (k, 0) if axis == "y" else (0, k)


def ring_others(own, axis, flip=False):
    return [fetch(own, *step(axis, k), flip) for k in (1, 2, 3)]


def ring_near(own, axis):
    return fetch(own, *step(axis, 1)), fetch(own, *step(axis, 3))


def ring_far(near, axis):
    up, down = near
    half = up.shape[0] // 2
    return fetch(up[:half], *step(axis, 1)), fetch(down[half:], *step(axis, 3))


def sum_pairs(value):
    for bit in (1, 2, 4, 8, 16):
        value = value + lax.ppermute(value, "expert", [(i ^ bit, i) for i in range(2 * SIDE * SIDE)])
    return value


def sum_dp(own):
    one, two, three = (fetch_dp(own, k) for k in (1, 2, 3))
    return (own + two) + (one + three)


def scatter_axis(chunks, axis):
    total = chunks[0].astype(F32)
    for k in (1, 2, 3):
        total = total + fetch(chunks[k], *step(axis, (SIDE - k) % SIDE)).astype(F32)
    return total.astype(BF16)


WHOLE = [(k, 0, SIDE) for k in range(SIDE)]
RELAYED = [(0, 0, SIDE), (1, 0, SIDE), (2, 0, 2), (2, 2, SIDE), (3, 0, SIDE)]


def layout_of(pieces):
    return WHOLE if len(pieces) == 2 * len(WHOLE) else RELAYED


def piece_copies(pieces, buf, sems, rows, lanes=None):
    layout = layout_of(pieces)
    count = len(layout)
    copies = []
    for i, piece in enumerate(pieces):
        k, low, high = layout[i % count]
        if lanes is None:
            half = buf.shape[3] // 2
            source = piece.at[:, rows]
            if i < count:
                target = buf.at[k, low:high, :, pl.ds(0, half)]
            else:
                target = buf.at[low:high, k, :, pl.ds(half, half)]
        else:
            source = piece.at[:, rows, pl.ds(0, lanes)]
            target = buf[0].at[k, low:high] if i < count else buf[1].at[low:high, k]
        copies.append(pltpu.make_async_copy(source, target, sems.at[i]))
    return copies


def route(first, ids_v, probs_v, rows_ref):
    tok = ids_v.shape[3]
    line = lax.broadcasted_iota(jnp.int32, (8, tok), 0)
    earlier = lax.broadcasted_iota(jnp.int32, (tok, tok), 0) < lax.broadcasted_iota(jnp.int32, (tok, tok), 1)
    earlier = jnp.where(earlier, 1.0, 0.0).astype(BF16)

    def body(b, carry):
        ids = ids_v[b // SIDE, b % SIDE].astype(F32)
        probs = probs_v[b // SIDE, b % SIDE].astype(F32)
        routed, weights = [], []
        for e in range(2):
            hit = ids == first + e
            routed.append(jnp.max(jnp.where(hit, 1.0, 0.0), axis=0, keepdims=True))
            weights.append(jnp.sum(jnp.where(hit, probs, 0.0), axis=0, keepdims=True))
        both = jnp.where(line == 0, routed[0], jnp.where(line == 1, routed[1], 0.0))
        slot = dot(both.astype(BF16), earlier, NN) + jnp.where(line == 1, 32.0, 0.0)
        slot = jnp.where(both > 0.5, slot, -1.0)
        rows_ref[b] = jnp.where(line < 2, slot, jnp.where(line == 2, weights[0], jnp.where(line == 3, weights[1], 0.0)))
        return carry

    lax.fori_loop(0, SIDE * SIDE, body, 0)


def slot_match(rows_ref, b, weighted):
    rows = rows_ref[b]
    slot = lax.broadcasted_iota(jnp.int32, (64, rows.shape[1]), 0).astype(F32)
    if weighted:
        picked = jnp.where(slot == rows[0:1], rows[2:3], jnp.where(slot == rows[1:2], rows[3:4], 0.0))
    else:
        picked = jnp.where((slot == rows[0:1]) | (slot == rows[1:2]), 1.0, 0.0)
    return picked.astype(BF16)


def gather_rows(rows_ref, buf, dest, weighted):
    def body(b, carry):
        picked = slot_match(rows_ref, b, weighted)
        out = dot(picked, buf[b // SIDE, b % SIDE], NN).astype(BF16)
        dest[0, b] = out[0:32]
        dest[1, b] = out[32:64]
        return carry

    lax.fori_loop(0, SIDE * SIDE, body, 0)


TILE = 8


def tile_rows(ref, e, m):
    part = ref[e, pl.ds(m * TILE, TILE)]
    return part.reshape(TILE * part.shape[1], part.shape[2])


def forward_kernel(count, mixing, *refs):
    pieces, (first_ref, gate_h, up_h, down_h, adn_ref, aup_ref) = refs[:count], refs[count : count + 6]
    out_h, rows_h, low_ref, act_h, route_ref = refs[count + 6 : count + 11]
    buf, ids_v, probs_v, gate_v, up_v, down_v, rows_v, res_v, act_v, sems, isems, wsems, osems = refs[count + 11 :]
    tok = buf.shape[2]
    infos = piece_copies(pieces, (ids_v, probs_v), isems, pl.ds(tok, 8), tok)
    loads = piece_copies(pieces, buf, sems, pl.ds(0, tok))
    for c in infos + loads:
        c.start()
    weights = []
    for e in range(2):
        weights.append(
            [
                pltpu.make_async_copy(gate_h.at[e], gate_v.at[e], wsems.at[e, 0]),
                pltpu.make_async_copy(up_h.at[e], up_v.at[e], wsems.at[e, 1]),
                pltpu.make_async_copy(down_h.at[e], down_v.at[e], wsems.at[e, 2]),
            ]
        )
        for c in weights[e]:
            c.start()
    for c in infos:
        c.wait()
    route(first_ref[0], ids_v, probs_v, route_ref)
    for c in loads:
        c.wait()
    gather_rows(route_ref, buf, rows_v, False)
    save_rows = pltpu.make_async_copy(rows_v, rows_h, osems.at[0])
    save_rows.start()
    saves = [save_rows]
    for e in range(2):
        for c in weights[e]:
            c.wait()

        def body(m, carry, e=e):
            data = tile_rows(rows_v, e, m)
            low = dot(data, adn_ref[e], NT).astype(BF16)
            low_ref[e, m] = low
            gate = dot(data, gate_v[e], NN) + dot(low, aup_ref[e], NN)
            up = dot(data, up_v[e], NN)
            sig = 1.0 / (1.0 + jnp.exp(-gate))
            hidden = (gate * sig * up).astype(BF16)
            act_v[e, m] = up * sig * (1.0 + gate * (1.0 - sig))
            res = dot(hidden, down_v[e], NN).astype(BF16)
            res_v[e, pl.ds(m * TILE, TILE)] = res.reshape(TILE, 32, res.shape[1])
            return carry

        lax.fori_loop(0, SIDE * SIDE // TILE, body, 0)
        save_act = pltpu.make_async_copy(act_v.at[e], act_h.at[e], osems.at[1 + e])
        save_act.start()
        saves.append(save_act)
        if not mixing:
            save_res = pltpu.make_async_copy(res_v.at[e], out_h.at[e], osems.at[3 + e])
            save_res.start()
            saves.append(save_res)
    for dy in range(SIDE if mixing else 0):

        def body(dx, carry, dy=dy):
            buf[dy, dx] = mix(route_ref, res_v, dy * SIDE + dx).astype(BF16)
            return carry

        lax.fori_loop(0, SIDE, body, 0)
        save = pltpu.make_async_copy(buf.at[dy], out_h.at[dy], osems.at[3 + dy])
        save.start()
        saves.append(save)
    for c in saves:
        c.wait()


def mix(route_ref, res_v, b):
    picked = slot_match(route_ref, b, True)
    return dot(picked, jnp.concatenate([res_v[0, b], res_v[1, b]], axis=0), TN)


def forward_call(pieces, tok, first, gate, up, down, adn, aup, mixing):
    width = 2 * pieces[0].shape[2]
    ff, rank = gate.shape[2], adn.shape[1]
    any_spec = pl.BlockSpec(memory_space=pl.ANY)
    vmem = pl.BlockSpec(memory_space=pltpu.VMEM)
    smem = pl.BlockSpec(memory_space=pltpu.SMEM)
    nb = SIDE * SIDE
    tiles, tile = nb // TILE, TILE * 32
    count = len(pieces)
    out = (SIDE, SIDE, tok, width) if mixing else (2, nb, 32, width)
    return pl.pallas_call(
        lambda *refs: forward_kernel(count, mixing, *refs),
        out_shape=(
            jax.ShapeDtypeStruct(out, BF16),
            jax.ShapeDtypeStruct((2, nb, 32, width), BF16),
            jax.ShapeDtypeStruct((2, tiles, tile, rank), BF16),
            jax.ShapeDtypeStruct((2, tiles, tile, ff), F32),
            jax.ShapeDtypeStruct((nb, 8, tok), F32),
        ),
        in_specs=[any_spec] * count + [smem] + [any_spec] * 3 + [vmem] * 2,
        out_specs=(any_spec, any_spec, vmem, any_spec, vmem),
        scratch_shapes=[
            pltpu.VMEM((SIDE, SIDE, tok, width), BF16),
            pltpu.VMEM((SIDE, SIDE, 8, tok), BF16),
            pltpu.VMEM((SIDE, SIDE, 8, tok), BF16),
            pltpu.VMEM((2, width, ff), BF16),
            pltpu.VMEM((2, width, ff), BF16),
            pltpu.VMEM((2, ff, width), BF16),
            pltpu.VMEM((2, nb, 32, width), BF16),
            pltpu.VMEM((2, nb, 32, width), BF16),
            pltpu.VMEM((2, tiles, tile, ff), F32),
            pltpu.SemaphoreType.DMA((count,)),
            pltpu.SemaphoreType.DMA((count,)),
            pltpu.SemaphoreType.DMA((2, 3)),
            pltpu.SemaphoreType.DMA((7,)),
        ],
        compiler_params=pltpu.CompilerParams(vmem_limit_bytes=60 * 1024 * 1024),
        cost_estimate=pl.CostEstimate(
            flops=2 * nb * 64 * width * (3 * ff + 256), transcendentals=nb * 64 * ff, bytes_accessed=50_000_000
        ),
        name="expert_forward",
    )(*pieces, first, gate, up, down, adn, aup)


def mix_kernel(route_ref, res_h, back_h, *refs):
    chunks, (buf, res_v, rsems, bsems, osems) = refs[: 2 * SIDE], refs[2 * SIDE :]
    half = buf.shape[3] // 2
    loads = [pltpu.make_async_copy(res_h.at[e], res_v.at[e], rsems.at[e]) for e in range(2)]
    backs = [pltpu.make_async_copy(back_h.at[dy], buf.at[dy], bsems.at[dy]) for dy in range(SIDE)]
    for c in loads + backs:
        c.start()
    for c in loads:
        c.wait()
    saves = []
    for dy in range(SIDE):
        backs[dy].wait()

        def body(dx, carry, dy=dy):
            buf[dy, dx] = (mix(route_ref, res_v, dy * SIDE + dx) + buf[dy, dx].astype(F32)).astype(BF16)
            return carry

        lax.fori_loop(0, SIDE, body, 0)
        saves.append(pltpu.make_async_copy(buf.at[dy, :, :, pl.ds(0, half)], chunks[dy], osems.at[dy]))
        saves[-1].start()
    for dx in range(SIDE):
        saves.append(
            pltpu.make_async_copy(buf.at[:, dx, :, pl.ds(half, half)], chunks[SIDE + dx], osems.at[SIDE + dx])
        )
        saves[-1].start()
    for c in saves:
        c.wait()


def mix_call(route_rows, res, back):
    any_spec = pl.BlockSpec(memory_space=pl.ANY)
    vmem = pl.BlockSpec(memory_space=pltpu.VMEM)
    tok, width = back.shape[2:]
    chunk = jax.ShapeDtypeStruct((SIDE, tok, width // 2), BF16)
    return pl.pallas_call(
        mix_kernel,
        out_shape=(chunk,) * (2 * SIDE),
        in_specs=[vmem, any_spec, any_spec],
        out_specs=(any_spec,) * (2 * SIDE),
        scratch_shapes=[
            pltpu.VMEM(back.shape, BF16),
            pltpu.VMEM(res.shape, BF16),
            pltpu.SemaphoreType.DMA((2,)),
            pltpu.SemaphoreType.DMA((SIDE,)),
            pltpu.SemaphoreType.DMA((2 * SIDE,)),
        ],
        compiler_params=pltpu.CompilerParams(vmem_limit_bytes=60 * 1024 * 1024),
        cost_estimate=pl.CostEstimate(
            flops=2 * SIDE * SIDE * 64 * tok * width, transcendentals=0, bytes_accessed=21_000_000
        ),
        name="expert_mix",
    )(route_rows, res, back)


def backward_kernel(final, *refs):
    pieces, (rows_ref, down_h, aup_ref, rows_h, low_ref, act_h) = refs[:8], refs[8:14]
    rest = refs[14:]
    if final:
        adn0_ref, aup0_ref, sd_ref, fdt_ref, sx_ref, fut_ref = rest[:6]
        gfd_ref, gfu_ref, gsd_ref, gsu_ref = rest[6:10]
        gadn, gaup, rest = rest[10], rest[11], rest[12:]
    else:
        gadn, gaup, rest = rest[0], rest[1], rest[2:]
    buf, down_v, rows_v, grad_v, act_v, sems, wsems = rest
    loads = piece_copies(pieces, buf, sems, pl.ds(0, buf.shape[2]))
    for c in loads:
        c.start()
    more = []
    for e in range(2):
        more.append(
            [
                pltpu.make_async_copy(down_h.at[e], down_v.at[e], wsems.at[e, 0]),
                pltpu.make_async_copy(act_h.at[e], act_v.at[e], wsems.at[e, 1]),
                pltpu.make_async_copy(rows_h.at[e], rows_v.at[e], wsems.at[e, 2]),
            ]
        )
        for c in more[e]:
            c.start()
    if final:
        gadn[...] = adn0_ref[...]
        gaup[...] = aup0_ref[...]
    else:
        gadn[...] = jnp.zeros(gadn.shape, F32)
        gaup[...] = jnp.zeros(gaup.shape, F32)
    for c in loads:
        c.wait()
    gather_rows(rows_ref, buf, grad_v, True)
    for e in range(2):
        for c in more[e]:
            c.wait()

        def body(m, carry, e=e):
            weighted = tile_rows(grad_v, e, m)
            data = tile_rows(rows_v, e, m)
            grad_hidden = dot(weighted, down_v[e], NT)
            grad_gate = (grad_hidden * act_v[e, m]).astype(BF16)
            grad_low = dot(grad_gate, aup_ref[e], NT).astype(BF16)
            gaup[e] += dot(low_ref[e, m], grad_gate, TN)
            gadn[e] += dot(grad_low, data, TN)
            return carry

        lax.fori_loop(0, SIDE * SIDE // TILE, body, 0)
    if not final:
        return
    kron = fdt_ref.shape[1]
    dn, up = fdt_ref.shape[2], fut_ref.shape[2]
    wide, quarter = fdt_ref.shape[3], fut_ref.shape[3] // kron
    gsd_ref[...] = jnp.zeros(gsd_ref.shape, F32)
    gsu_ref[...] = jnp.zeros(gsu_ref.shape, F32)
    for e in range(2):
        for i in range(kron):
            factor = fdt_ref[e, i]
            total = jnp.zeros((dn, wide), F32)
            for a in range(kron):
                for c in range(kron):
                    block = gadn[e, c * dn : (c + 1) * dn, a * wide : (a + 1) * wide]
                    place = (i * kron + a) * kron + c
                    total = total + sd_ref[place] * block
                    line = jnp.sum(factor * block, axis=0, keepdims=True)
                    short = line[:, 0:128]
                    for w in range(128, wide, 128):
                        short = short + line[:, w : w + 128]
                    gsd_ref[place : place + 1] += short
            gfd_ref[e, i] = total
            factor = fut_ref[e, i]
            total = jnp.zeros(factor.shape, F32)
            for a in range(kron):
                block = gaup[e, a * up : (a + 1) * up]
                place = i * kron + a
                total = total + sx_ref[place : place + 1] * block
                gsu_ref[place : place + 1] += jnp.sum(factor * block, axis=0, keepdims=True)
            folded = total[:, 0:quarter]
            for c in range(1, kron):
                folded = folded + total[:, c * quarter : (c + 1) * quarter]
            gfu_ref[e, i] = folded


def backward_call(pieces, rows, down, aup, stash, tail=None):
    tok, width = pieces[0].shape[1], 2 * pieces[0].shape[2]
    ff, rank = down.shape[1], aup.shape[1]
    any_spec = pl.BlockSpec(memory_space=pl.ANY)
    vmem = pl.BlockSpec(memory_space=pltpu.VMEM)
    nb = SIDE * SIDE
    tiles, tile = nb // TILE, TILE * 32
    saved_rows, saved_low, saved_act = stash
    args = [*pieces, rows, down, aup, saved_rows, saved_low, saved_act]
    in_specs = [any_spec] * 8 + [vmem, any_spec, vmem, any_spec, vmem, any_spec]
    sums = [(2, rank, width), (2, rank, ff)]
    scratch = []
    if tail is None:
        out_shape = tuple(jax.ShapeDtypeStruct(s, F32) for s in sums)
    else:
        (adn0, aup0), share_down, fdt, sx, fut = tail
        kron = fdt.shape[1]
        args += [adn0, aup0, share_down.reshape(-1), fdt, sx, fut]
        in_specs += [vmem, vmem, pl.BlockSpec(memory_space=pltpu.SMEM), vmem, vmem, vmem]
        out_shape = (
            jax.ShapeDtypeStruct(fdt.shape, F32),
            jax.ShapeDtypeStruct(fut.shape[:3] + (ff // kron,), F32),
            jax.ShapeDtypeStruct((kron**3, 128), F32),
            jax.ShapeDtypeStruct((kron**2, ff), F32),
        )
        scratch = [pltpu.VMEM(s, F32) for s in sums]
    return pl.pallas_call(
        lambda *refs: backward_kernel(tail is not None, *refs),
        out_shape=out_shape,
        in_specs=in_specs,
        out_specs=tuple(vmem for _ in out_shape),
        scratch_shapes=scratch
        + [
            pltpu.VMEM((SIDE, SIDE, tok, width), BF16),
            pltpu.VMEM((2, ff, width), BF16),
            pltpu.VMEM((2, nb, 32, width), BF16),
            pltpu.VMEM((2, nb, 32, width), BF16),
            pltpu.VMEM((2, tiles, tile, ff), F32),
            pltpu.SemaphoreType.DMA((8,)),
            pltpu.SemaphoreType.DMA((2, 3)),
        ],
        compiler_params=pltpu.CompilerParams(vmem_limit_bytes=60 * 1024 * 1024),
        cost_estimate=pl.CostEstimate(
            flops=2 * nb * 64 * width * (ff + 256), transcendentals=0, bytes_accessed=30_000_000
        ),
        name="expert_backward" if tail is None else "expert_backward_last",
    )(*args)


def layer(
    tokens,
    grad_mixed,
    expert_ids,
    gate_probs,
    gate_proj,
    up_proj,
    down_proj,
    share_down,
    share_up,
    factor_down,
    factor_up,
):
    tok, width = tokens.shape
    half = width // 2
    kron = share_down.shape[0]
    local = gate_proj.shape[0]
    ff = gate_proj.shape[2]
    first_expert = lax.axis_index("expert") * local

    highest = lax.Precision.HIGHEST
    adn = jnp.einsum("iac,eibd->ecdab", share_down, factor_down, precision=highest)
    adn = adn.reshape(local, -1, width).astype(BF16)
    aup = jnp.einsum("iac,eibd->eabcd", share_up, factor_up, precision=highest)
    aup = aup.reshape(local, -1, ff).astype(BF16)
    fdt = factor_down.transpose(0, 1, 3, 2)
    fut = jnp.tile(factor_up, (1, 1, 1, kron))
    sx = jnp.repeat(share_up, ff // kron, axis=2).reshape(kron * kron, ff)

    free = jnp.zeros((8, half - tok), BF16)
    info = jnp.concatenate([expert_ids.T.astype(BF16), free, gate_probs.T, free], axis=1)
    block = jnp.concatenate([grad_mixed, tokens, info], axis=0)
    own = fetch(block, 0, 0, True)
    left = [own[:, :half], *ring_others(block[:, :half], "x", True)]
    right = [own[:, half:], *ring_others(block[:, half:], "y", True)]
    tok_left, tok_right = (jnp.stack([v[tok:] for v in side]) for side in (left, right))
    grad_left, grad_right = (jnp.stack([v[:tok] for v in side]) for side in (left, right))

    near_left, near_right = ring_near(tok_left, "y"), ring_near(tok_right, "x")
    far_left, far_right = ring_far(near_left, "y"), ring_far(near_right, "x")
    tok_cross = [tok_left, near_left[0], *far_left, near_left[1], tok_right, near_right[0], *far_right, near_right[1]]
    tied = lax.optimization_barrier((grad_left, grad_right, *tok_cross))
    (grad_left, grad_right), tok_cross = tied[:2], list(tied[2:])
    tok_own = [fetch(p, 0, 0, True) for p in tok_cross]
    grad_cross = [grad_left, *ring_others(grad_left, "y"), grad_right, *ring_others(grad_right, "x")]
    grad_own = [fetch(p, 0, 0, True) for p in grad_cross]

    first = first_expert.astype(F32).reshape(1)
    weights = (gate_proj, up_proj, down_proj, adn, aup)
    part_cross, *stash_cross, rows_cross = forward_call(tok_cross, tok, first, *weights, True)
    part_back = fetch(part_cross, 0, 0, True)
    res_own, *stash_own, rows_own = forward_call(tok_own, tok, first, *weights, False)
    chunks = mix_call(rows_own, res_own, part_back)

    out_a = scatter_axis(chunks[:SIDE], "y")
    out_b = scatter_axis(chunks[SIDE:], "x")
    out_a = scatter_axis([out_a[k] for k in range(SIDE)], "x")
    out_b = scatter_axis([out_b[k] for k in range(SIDE)], "y")
    mixed = jnp.concatenate([out_a, out_b], axis=1)

    sums = backward_call(grad_cross, rows_cross, down_proj, aup, stash_cross)
    gfd, gfu, gsd, gsu = backward_call(grad_own, rows_own, down_proj, aup, stash_own, (sums, share_down, fdt, sx, fut))
    gsd = jnp.sum(gsd, axis=1)
    gsu = jnp.sum(gsu.reshape(kron**3, ff // kron), axis=1)
    shares = jnp.concatenate([gsd, gsu]).reshape(1, -1)
    shape_fd, shape_fu = gfd.shape, gfu.shape
    packed = jnp.concatenate([gfd.reshape(-1, 128), gfu.reshape(-1, 128), shares], axis=0)
    packed = sum_dp(packed)
    cut = gfd.size // 128
    gfd = packed[:cut].reshape(shape_fd)
    gfu = packed[cut:-1].reshape(shape_fu)
    shares = sum_pairs(packed[-1:])
    shares = shares.reshape(2, kron, kron, kron)
    return (mixed, gfd.transpose(0, 1, 3, 2), gfu, shares[0], shares[1])


def solution(mesh):
    step = shard_map_step(mesh)
    return step


def shard_map_step(mesh):
    return jax.shard_map(
        layer,
        mesh=mesh,
        in_specs=(
            P(("dp", "expert"), None),
            P(("dp", "expert"), None),
            P(("dp", "expert"), None),
            P(("dp", "expert"), None),
            P("expert", None, None),
            P("expert", None, None),
            P("expert", None, None),
            P(),
            P(),
            P("expert", None, None, None),
            P("expert", None, None, None),
        ),
        out_specs=(
            P(("dp", "expert"), None),
            P("expert", None, None, None),
            P("expert", None, None, None),
            P(),
            P(),
        ),
        check_vma=False,
    )
```

```python
import jax
import jax.numpy as jnp
from jax import lax
from jax.experimental import pallas as pl
from jax.experimental.pallas import tpu as pltpu
from jax.sharding import PartitionSpec as P


F32 = jnp.float32
BF16 = jnp.bfloat16
SIDE = 4
NT = (((1,), (1,)), ((), ()))
TN = (((0,), (0,)), ((), ()))
NN = (((1,), (0,)), ((), ()))


def dot(a, b, dims):
    return lax.dot_general(a, b, dims, preferred_element_type=F32)


def fetch(value, dy, dx, flip=False):
    perm = []
    for y in range(SIDE):
        for x in range(SIDE):
            for c in range(2):
                source = (((y + dy) % SIDE) * SIDE + (x + dx) % SIDE) * 2 + (c ^ int(flip))
                perm.append((source, (y * SIDE + x) * 2 + c))
    return lax.ppermute(value, "expert", perm)


def fetch_dp(value, shift):
    return lax.ppermute(value, "dp", [((z + shift) % SIDE, z) for z in range(SIDE)])


def step(axis, k):
    return (k, 0) if axis == "y" else (0, k)


def ring_others(own, axis, flip=False):
    return [fetch(own, *step(axis, k), flip) for k in (1, 2, 3)]


def sum_ring(own, axis):
    one, two, three = ring_others(own, axis)
    return (own + two) + (one + three)


def sum_dp(own):
    one, two, three = (fetch_dp(own, k) for k in (1, 2, 3))
    return (own + two) + (one + three)


def scatter_axis(chunks, axis):
    total = chunks[0].astype(F32)
    for k in (1, 2, 3):
        total = total + fetch(chunks[k], *step(axis, (SIDE - k) % SIDE)).astype(F32)
    return total.astype(BF16)


WHOLE = [(k, 0, SIDE) for k in range(SIDE)]
RELAYED = [(0, 0, SIDE)] + [(k, 2 * h, 2 * h + 2) for k in (1, 2, 3) for h in (0, 1)]


def layout_of(pieces):
    return WHOLE if len(pieces) == 2 * len(WHOLE) else RELAYED


def piece_copies(pieces, buf, sems, rows, lanes=None):
    layout = layout_of(pieces)
    count = len(layout)
    copies = []
    for i, piece in enumerate(pieces):
        k, low, high = layout[i % count]
        if lanes is None:
            half = buf.shape[3] // 2
            source = piece.at[:, rows]
            if i < count:
                target = buf.at[k, low:high, :, pl.ds(0, half)]
            else:
                target = buf.at[low:high, k, :, pl.ds(half, half)]
        else:
            source = piece.at[:, rows, pl.ds(0, lanes)]
            target = buf[0].at[k, low:high] if i < count else buf[1].at[low:high, k]
        copies.append(pltpu.make_async_copy(source, target, sems.at[i]))
    return copies


def route(first, ids_v, probs_v, rows_ref):
    tok = ids_v.shape[3]
    line = lax.broadcasted_iota(jnp.int32, (8, tok), 0)
    earlier = lax.broadcasted_iota(jnp.int32, (tok, tok), 0) < lax.broadcasted_iota(jnp.int32, (tok, tok), 1)
    earlier = jnp.where(earlier, 1.0, 0.0).astype(BF16)

    def body(b, carry):
        ids = ids_v[b // SIDE, b % SIDE].astype(F32)
        probs = probs_v[b // SIDE, b % SIDE].astype(F32)
        routed, weights = [], []
        for e in range(2):
            hit = ids == first + e
            routed.append(jnp.max(jnp.where(hit, 1.0, 0.0), axis=0, keepdims=True))
            weights.append(jnp.sum(jnp.where(hit, probs, 0.0), axis=0, keepdims=True))
        both = jnp.where(line == 0, routed[0], jnp.where(line == 1, routed[1], 0.0))
        slot = dot(both.astype(BF16), earlier, NN) + jnp.where(line == 1, 32.0, 0.0)
        slot = jnp.where(both > 0.5, slot, -1.0)
        rows_ref[b] = jnp.where(line < 2, slot, jnp.where(line == 2, weights[0], jnp.where(line == 3, weights[1], 0.0)))
        return carry

    lax.fori_loop(0, SIDE * SIDE, body, 0)


def slot_match(rows_ref, b, weighted):
    rows = rows_ref[b]
    slot = lax.broadcasted_iota(jnp.int32, (64, rows.shape[1]), 0).astype(F32)
    if weighted:
        picked = jnp.where(slot == rows[0:1], rows[2:3], jnp.where(slot == rows[1:2], rows[3:4], 0.0))
    else:
        picked = jnp.where((slot == rows[0:1]) | (slot == rows[1:2]), 1.0, 0.0)
    return picked.astype(BF16)


def gather_rows(rows_ref, buf, dest, weighted):
    def body(b, carry):
        picked = slot_match(rows_ref, b, weighted)
        out = dot(picked, buf[b // SIDE, b % SIDE], NN).astype(BF16)
        dest[0, b] = out[0:32]
        dest[1, b] = out[32:64]
        return carry

    lax.fori_loop(0, SIDE * SIDE, body, 0)


TILE = 8


def tile_rows(ref, e, m):
    part = ref[e, pl.ds(m * TILE, TILE)]
    return part.reshape(TILE * part.shape[1], part.shape[2])


def forward_kernel(count, mixing, *refs):
    pieces, (first_ref, gate_h, up_h, down_h, adn_ref, aup_ref) = refs[:count], refs[count : count + 6]
    out_h, rows_h, low_ref, act_h, route_ref = refs[count + 6 : count + 11]
    buf, ids_v, probs_v, gate_v, up_v, down_v, rows_v, res_v, act_v, sems, isems, wsems, osems = refs[count + 11 :]
    tok = buf.shape[2]
    infos = piece_copies(pieces, (ids_v, probs_v), isems, pl.ds(tok, 8), tok)
    loads = piece_copies(pieces, buf, sems, pl.ds(0, tok))
    for c in infos + loads:
        c.start()

    def weight_copies(e):
        return [
            pltpu.make_async_copy(gate_h.at[e], gate_v.at[e], wsems.at[e, 0]),
            pltpu.make_async_copy(up_h.at[e], up_v.at[e], wsems.at[e, 1]),
            pltpu.make_async_copy(down_h.at[e], down_v.at[e], wsems.at[e, 2]),
        ]

    for e in range(2):
        for c in weight_copies(e):
            c.start()
    for c in infos:
        c.wait()
    route(first_ref[0], ids_v, probs_v, route_ref)
    for c in loads:
        c.wait()
    gather_rows(route_ref, buf, rows_v, False)
    save_rows = pltpu.make_async_copy(rows_v, rows_h, osems.at[0])
    save_rows.start()
    saves = [save_rows]
    tiles = SIDE * SIDE // TILE

    def save_copies(e):
        copies = [pltpu.make_async_copy(act_v.at[e], act_h.at[e], osems.at[1 + e])]
        if not mixing:
            copies.append(pltpu.make_async_copy(res_v.at[e], out_h.at[e], osems.at[3 + e]))
        return copies

    def body(i, carry):
        e, m = i // tiles, i % tiles

        @pl.when(m == 0)
        def _():
            for c in weight_copies(e):
                c.wait()

        data = tile_rows(rows_v, e, m)
        low = dot(data, adn_ref[e], NT).astype(BF16)
        low_ref[e, m] = low
        gate = dot(data, gate_v[e], NN) + dot(low, aup_ref[e], NN)
        up = dot(data, up_v[e], NN)
        sig = 1.0 / (1.0 + jnp.exp(-gate))
        hidden = (gate * sig * up).astype(BF16)
        act_v[e, m] = up * sig * (1.0 + gate * (1.0 - sig))
        res = dot(hidden, down_v[e], NN).astype(BF16)
        res_v[e, pl.ds(m * TILE, TILE)] = res.reshape(TILE, 32, res.shape[1])

        @pl.when(m == tiles - 1)
        def _():
            for c in save_copies(e):
                c.start()

        return carry

    lax.fori_loop(0, 2 * tiles, body, 0)
    saves += save_copies(0) + save_copies(1)
    for dy in range(SIDE if mixing else 0):

        def body(dx, carry, dy=dy):
            buf[dy, dx] = mix(route_ref, res_v, dy * SIDE + dx).astype(BF16)
            return carry

        lax.fori_loop(0, SIDE, body, 0)
        save = pltpu.make_async_copy(buf.at[dy], out_h.at[dy], osems.at[3 + dy])
        save.start()
        saves.append(save)
    for c in saves:
        c.wait()


def mix(route_ref, res_v, b):
    picked = slot_match(route_ref, b, True)
    return dot(picked, jnp.concatenate([res_v[0, b], res_v[1, b]], axis=0), TN)


def forward_call(pieces, tok, first, gate, up, down, adn, aup, mixing):
    width = 2 * pieces[0].shape[2]
    ff, rank = gate.shape[2], adn.shape[1]
    any_spec = pl.BlockSpec(memory_space=pl.ANY)
    vmem = pl.BlockSpec(memory_space=pltpu.VMEM)
    smem = pl.BlockSpec(memory_space=pltpu.SMEM)
    nb = SIDE * SIDE
    tiles, tile = nb // TILE, TILE * 32
    count = len(pieces)
    out = (SIDE, SIDE, tok, width) if mixing else (2, nb, 32, width)
    return pl.pallas_call(
        lambda *refs: forward_kernel(count, mixing, *refs),
        out_shape=(
            jax.ShapeDtypeStruct(out, BF16),
            jax.ShapeDtypeStruct((2, nb, 32, width), BF16),
            jax.ShapeDtypeStruct((2, tiles, tile, rank), BF16),
            jax.ShapeDtypeStruct((2, tiles, tile, ff), F32),
            jax.ShapeDtypeStruct((nb, 8, tok), F32),
        ),
        in_specs=[any_spec] * count + [smem] + [any_spec] * 3 + [vmem] * 2,
        out_specs=(any_spec, any_spec, vmem, any_spec, vmem),
        scratch_shapes=[
            pltpu.VMEM((SIDE, SIDE, tok, width), BF16),
            pltpu.VMEM((SIDE, SIDE, 8, tok), BF16),
            pltpu.VMEM((SIDE, SIDE, 8, tok), BF16),
            pltpu.VMEM((2, width, ff), BF16),
            pltpu.VMEM((2, width, ff), BF16),
            pltpu.VMEM((2, ff, width), BF16),
            pltpu.VMEM((2, nb, 32, width), BF16),
            pltpu.VMEM((2, nb, 32, width), BF16),
            pltpu.VMEM((2, tiles, tile, ff), F32),
            pltpu.SemaphoreType.DMA((count,)),
            pltpu.SemaphoreType.DMA((count,)),
            pltpu.SemaphoreType.DMA((2, 3)),
            pltpu.SemaphoreType.DMA((7,)),
        ],
        compiler_params=pltpu.CompilerParams(vmem_limit_bytes=60 * 1024 * 1024),
        cost_estimate=pl.CostEstimate(
            flops=2 * nb * 64 * width * (3 * ff + 256), transcendentals=nb * 64 * ff, bytes_accessed=50_000_000
        ),
        name="expert_forward",
    )(*pieces, first, gate, up, down, adn, aup)


def mix_kernel(route_ref, res_h, back_h, *refs):
    chunks, (buf, res_v, rsems, bsems, osems) = refs[: 2 * SIDE], refs[2 * SIDE :]
    half = buf.shape[3] // 2
    loads = [pltpu.make_async_copy(res_h.at[e], res_v.at[e], rsems.at[e]) for e in range(2)]
    backs = [pltpu.make_async_copy(back_h.at[dy], buf.at[dy], bsems.at[dy]) for dy in range(SIDE)]
    for c in loads + backs:
        c.start()
    for c in loads:
        c.wait()
    saves = []
    for dy in range(SIDE):
        backs[dy].wait()

        def body(dx, carry, dy=dy):
            buf[dy, dx] = (mix(route_ref, res_v, dy * SIDE + dx) + buf[dy, dx].astype(F32)).astype(BF16)
            return carry

        lax.fori_loop(0, SIDE, body, 0)
        saves.append(pltpu.make_async_copy(buf.at[dy, :, :, pl.ds(0, half)], chunks[dy], osems.at[dy]))
        saves[-1].start()
    for dx in range(SIDE):
        saves.append(
            pltpu.make_async_copy(buf.at[:, dx, :, pl.ds(half, half)], chunks[SIDE + dx], osems.at[SIDE + dx])
        )
        saves[-1].start()
    for c in saves:
        c.wait()


def mix_call(route_rows, res, back):
    any_spec = pl.BlockSpec(memory_space=pl.ANY)
    vmem = pl.BlockSpec(memory_space=pltpu.VMEM)
    tok, width = back.shape[2:]
    chunk = jax.ShapeDtypeStruct((SIDE, tok, width // 2), BF16)
    return pl.pallas_call(
        mix_kernel,
        out_shape=(chunk,) * (2 * SIDE),
        in_specs=[vmem, any_spec, any_spec],
        out_specs=(any_spec,) * (2 * SIDE),
        scratch_shapes=[
            pltpu.VMEM(back.shape, BF16),
            pltpu.VMEM(res.shape, BF16),
            pltpu.SemaphoreType.DMA((2,)),
            pltpu.SemaphoreType.DMA((SIDE,)),
            pltpu.SemaphoreType.DMA((2 * SIDE,)),
        ],
        compiler_params=pltpu.CompilerParams(vmem_limit_bytes=60 * 1024 * 1024),
        cost_estimate=pl.CostEstimate(
            flops=2 * SIDE * SIDE * 64 * tok * width, transcendentals=0, bytes_accessed=21_000_000
        ),
        name="expert_mix",
    )(route_rows, res, back)


def backward_kernel(final, *refs):
    pieces, (rows_ref, down_h, aup_ref, rows_h, low_ref, act_h) = refs[:8], refs[8:14]
    rest = refs[14:]
    if final:
        adn0_ref, aup0_ref, sd_ref, fdt_ref, sx_ref, fut_ref = rest[:6]
        gfd_ref, gfu_ref, gsd_ref, gsu_ref = rest[6:10]
        gadn, gaup, rest = rest[10], rest[11], rest[12:]
    else:
        gadn, gaup, rest = rest[0], rest[1], rest[2:]
    buf, down_v, rows_v, grad_v, act_v, sems, wsems = rest
    loads = piece_copies(pieces, buf, sems, pl.ds(0, buf.shape[2]))
    for c in loads:
        c.start()

    def more_copies(e):
        return [
            pltpu.make_async_copy(down_h.at[e], down_v.at[e], wsems.at[e, 0]),
            pltpu.make_async_copy(act_h.at[e], act_v.at[e], wsems.at[e, 1]),
            pltpu.make_async_copy(rows_h.at[e], rows_v.at[e], wsems.at[e, 2]),
        ]

    for e in range(2):
        for c in more_copies(e):
            c.start()
    if final:
        gadn[...] = adn0_ref[...]
        gaup[...] = aup0_ref[...]
    else:
        gadn[...] = jnp.zeros(gadn.shape, F32)
        gaup[...] = jnp.zeros(gaup.shape, F32)
    for c in loads:
        c.wait()
    gather_rows(rows_ref, buf, grad_v, True)
    tiles = SIDE * SIDE // TILE

    def body(i, carry):
        e, m = i // tiles, i % tiles

        @pl.when(m == 0)
        def _():
            for c in more_copies(e):
                c.wait()

        weighted = tile_rows(grad_v, e, m)
        data = tile_rows(rows_v, e, m)
        grad_hidden = dot(weighted, down_v[e], NT)
        grad_gate = (grad_hidden * act_v[e, m]).astype(BF16)
        grad_low = dot(grad_gate, aup_ref[e], NT).astype(BF16)
        gaup[e] += dot(low_ref[e, m], grad_gate, TN)
        gadn[e] += dot(grad_low, data, TN)
        return carry

    lax.fori_loop(0, 2 * tiles, body, 0)
    if not final:
        return
    kron = fdt_ref.shape[1]
    dn, up = fdt_ref.shape[2], fut_ref.shape[2]
    wide, quarter = fdt_ref.shape[3], fut_ref.shape[3] // kron
    gsd_ref[...] = jnp.zeros(gsd_ref.shape, F32)
    gsu_ref[...] = jnp.zeros(gsu_ref.shape, F32)
    for e in range(2):
        for i in range(kron):
            factor = fdt_ref[e, i]
            total = jnp.zeros((dn, wide), F32)
            for a in range(kron):
                for c in range(kron):
                    block = gadn[e, c * dn : (c + 1) * dn, a * wide : (a + 1) * wide]
                    place = (i * kron + a) * kron + c
                    total = total + sd_ref[place] * block
                    line = jnp.sum(factor * block, axis=0, keepdims=True)
                    short = line[:, 0:128]
                    for w in range(128, wide, 128):
                        short = short + line[:, w : w + 128]
                    gsd_ref[place : place + 1] += short
            gfd_ref[e, i] = total
            factor = fut_ref[e, i]
            total = jnp.zeros(factor.shape, F32)
            for a in range(kron):
                block = gaup[e, a * up : (a + 1) * up]
                place = i * kron + a
                total = total + sx_ref[place : place + 1] * block
                gsu_ref[place : place + 1] += jnp.sum(factor * block, axis=0, keepdims=True)
            folded = total[:, 0:quarter]
            for c in range(1, kron):
                folded = folded + total[:, c * quarter : (c + 1) * quarter]
            gfu_ref[e, i] = folded


def backward_call(pieces, rows, down, aup, stash, tail=None):
    tok, width = pieces[0].shape[1], 2 * pieces[0].shape[2]
    ff, rank = down.shape[1], aup.shape[1]
    any_spec = pl.BlockSpec(memory_space=pl.ANY)
    vmem = pl.BlockSpec(memory_space=pltpu.VMEM)
    nb = SIDE * SIDE
    tiles, tile = nb // TILE, TILE * 32
    saved_rows, saved_low, saved_act = stash
    args = [*pieces, rows, down, aup, saved_rows, saved_low, saved_act]
    in_specs = [any_spec] * 8 + [vmem, any_spec, vmem, any_spec, vmem, any_spec]
    sums = [(2, rank, width), (2, rank, ff)]
    scratch = []
    if tail is None:
        out_shape = tuple(jax.ShapeDtypeStruct(s, F32) for s in sums)
    else:
        (adn0, aup0), share_down, fdt, sx, fut = tail
        kron = fdt.shape[1]
        args += [adn0, aup0, share_down.reshape(-1), fdt, sx, fut]
        in_specs += [vmem, vmem, pl.BlockSpec(memory_space=pltpu.SMEM), vmem, vmem, vmem]
        out_shape = (
            jax.ShapeDtypeStruct(fdt.shape, F32),
            jax.ShapeDtypeStruct(fut.shape[:3] + (ff // kron,), F32),
            jax.ShapeDtypeStruct((kron**3, 128), F32),
            jax.ShapeDtypeStruct((kron**2, ff), F32),
        )
        scratch = [pltpu.VMEM(s, F32) for s in sums]
    return pl.pallas_call(
        lambda *refs: backward_kernel(tail is not None, *refs),
        out_shape=out_shape,
        in_specs=in_specs,
        out_specs=tuple(vmem for _ in out_shape),
        scratch_shapes=scratch
        + [
            pltpu.VMEM((SIDE, SIDE, tok, width), BF16),
            pltpu.VMEM((2, ff, width), BF16),
            pltpu.VMEM((2, nb, 32, width), BF16),
            pltpu.VMEM((2, nb, 32, width), BF16),
            pltpu.VMEM((2, tiles, tile, ff), F32),
            pltpu.SemaphoreType.DMA((8,)),
            pltpu.SemaphoreType.DMA((2, 3)),
        ],
        compiler_params=pltpu.CompilerParams(vmem_limit_bytes=60 * 1024 * 1024),
        cost_estimate=pl.CostEstimate(
            flops=2 * nb * 64 * width * (ff + 256), transcendentals=0, bytes_accessed=30_000_000
        ),
        name="expert_backward" if tail is None else "expert_backward_last",
    )(*args)


def layer(
    tokens,
    grad_mixed,
    expert_ids,
    gate_probs,
    gate_proj,
    up_proj,
    down_proj,
    share_down,
    share_up,
    factor_down,
    factor_up,
):
    tok, width = tokens.shape
    half = width // 2
    kron = share_down.shape[0]
    local = gate_proj.shape[0]
    ff = gate_proj.shape[2]
    first_expert = lax.axis_index("expert") * local

    highest = lax.Precision.HIGHEST
    adn = jnp.einsum("iac,eibd->ecdab", share_down, factor_down, precision=highest)
    adn = adn.reshape(local, -1, width).astype(BF16)
    aup = jnp.einsum("iac,eibd->eabcd", share_up, factor_up, precision=highest)
    aup = aup.reshape(local, -1, ff).astype(BF16)
    fdt = factor_down.transpose(0, 1, 3, 2)
    fut = jnp.tile(factor_up, (1, 1, 1, kron))
    sx = jnp.repeat(share_up, ff // kron, axis=2).reshape(kron * kron, ff)

    def phase_one(block):
        own = fetch(block, 0, 0, True)
        left = [own[:, :half], *ring_others(block[:, :half], "x", True)]
        right = [own[:, half:], *ring_others(block[:, half:], "y", True)]
        return left, right

    free = jnp.zeros((8, half - tok), BF16)
    info = jnp.concatenate([expert_ids.T.astype(BF16), free, gate_probs.T, free], axis=1)
    tok_sides = phase_one(jnp.concatenate([tokens, info], axis=0))
    halves = [[jnp.stack(side[2 * h : 2 * h + 2]) for h in (0, 1)] for side in tok_sides]
    grad_block, halves = lax.optimization_barrier((grad_mixed, halves))
    grad_sides = phase_one(grad_block)
    tok_left, tok_right = (jnp.concatenate(h, axis=0) for h in halves)
    grad_left, grad_right = (jnp.stack(side) for side in grad_sides)

    tok_cross = []
    for axis, whole, (low, high) in (("y", tok_left, halves[0]), ("x", tok_right, halves[1])):
        up_low, down_high = fetch(low, *step(axis, 1)), fetch(high, *step(axis, 3))
        up_high, down_low = fetch(high, *step(axis, 1)), fetch(low, *step(axis, 3))
        far_low, far_high = fetch(up_low, *step(axis, 1)), fetch(down_high, *step(axis, 3))
        tok_cross += [whole, up_low, up_high, far_low, far_high, down_low, down_high]
    tied = lax.optimization_barrier((grad_left, grad_right, *tok_cross))
    (grad_left, grad_right), tok_cross = tied[:2], list(tied[2:])
    tok_own = [fetch(p, 0, 0, True) for p in tok_cross]
    grad_cross = [grad_left, *ring_others(grad_left, "y"), grad_right, *ring_others(grad_right, "x")]
    grad_own = [fetch(p, 0, 0, True) for p in grad_cross]

    first = first_expert.astype(F32).reshape(1)
    weights = (gate_proj, up_proj, down_proj, adn, aup)
    part_cross, *stash_cross, rows_cross = forward_call(tok_cross, tok, first, *weights, True)
    part_back = fetch(part_cross, 0, 0, True)
    res_own, *stash_own, rows_own = forward_call(tok_own, tok, first, *weights, False)
    chunks = mix_call(rows_own, res_own, part_back)

    out_a = scatter_axis(chunks[:SIDE], "y")
    out_b = scatter_axis(chunks[SIDE:], "x")
    out_a = scatter_axis([out_a[k] for k in range(SIDE)], "x")
    out_b = scatter_axis([out_b[k] for k in range(SIDE)], "y")
    mixed = jnp.concatenate([out_a, out_b], axis=1)

    sums = backward_call(grad_cross, rows_cross, down_proj, aup, stash_cross)
    gfd, gfu, gsd, gsu = backward_call(grad_own, rows_own, down_proj, aup, stash_own, (sums, share_down, fdt, sx, fut))
    gsd = jnp.sum(gsd, axis=1)
    gsu = jnp.sum(gsu.reshape(kron**3, ff // kron), axis=1)
    shares = jnp.concatenate([gsd, gsu]).reshape(1, -1)
    shape_fd, shape_fu = gfd.shape, gfu.shape
    packed = jnp.concatenate([gfd.reshape(-1, 128), gfu.reshape(-1, 128), shares], axis=0)
    packed = sum_dp(packed)
    cut = gfd.size // 128
    gfd = packed[:cut].reshape(shape_fd)
    gfu = packed[cut:-1].reshape(shape_fu)
    shares = packed[-1:]
    shares = shares + fetch(shares, 0, 0, True)
    shares = sum_ring(sum_ring(shares, "x"), "y")
    shares = shares.reshape(2, kron, kron, kron)
    return (mixed, gfd.transpose(0, 1, 3, 2), gfu, shares[0], shares[1])


def solution(mesh):
    step = shard_map_step(mesh)
    return step


def shard_map_step(mesh):
    return jax.shard_map(
        layer,
        mesh=mesh,
        in_specs=(
            P(("dp", "expert"), None),
            P(("dp", "expert"), None),
            P(("dp", "expert"), None),
            P(("dp", "expert"), None),
            P("expert", None, None),
            P("expert", None, None),
            P("expert", None, None),
            P(),
            P(),
            P("expert", None, None, None),
            P("expert", None, None, None),
        ),
        out_specs=(
            P(("dp", "expert"), None),
            P("expert", None, None, None),
            P("expert", None, None, None),
            P(),
            P(),
        ),
        check_vma=False,
    )
```
